128 devices in a mesh: seq: 32 (over z, x, core), head: 4 (over y).
Axes of the slice: x: 4, y: 4, z: 4, core: 2. Of those that a mesh axis runs over, the one named last changes fastest.
Arguments:
- queries: bfloat16 [16384, 4096], P('seq', 'head'), may hold values from -6 to 6
- keys: bfloat16 [16384, 4096], P('seq', 'head'), may hold values from -6 to 6
- values: bfloat16 [16384, 4096], P('seq', 'head'), may hold values from -6 to 6
- log_decay: float32 [32, 16384], P('head', 'seq'), may hold values from -3 to 0
- beta: float32 [32, 16384], P('head', 'seq'), may hold values from 0.001 to 0.03
- level_weights: float32 [10, 32, 16384], P(None, 'head', 'seq'), may hold values from 0.25 to 2
- doc_start: int32 [256], P('seq'), may hold values from 0 to 1, as said below
- norm_gain: float32 [4096], P('head'), may hold values from 0.25 to 1.75
- out_weight: bfloat16 [4096, 4096], P('head'), may hold values from -0.09375 to 0.09375
Outputs:
- mixed: bfloat16 [16384, 4096], P(('seq', 'head'))
The draws below stay inside these ranges and needn't reach their ends.
Inputs may be any that keep to these rules, and one draw needn't show every extreme that they name: doc_start is 0 on the first 128 spans; the second half holds at least one 1.
All inputs are finite; a program needn't handle non-finite values.
Results may differ from the reference program's by a relative error of at most 0.014.
Values may be sent and summed in bfloat16 or wider, within the bound.
No kernel may reach another device: no remote copies, remote signals or barrier semaphores. Data moves between devices by JAX's collectives and lax.ppermute only.
A program may use at most 128 MiB of HBM per device.

```python
import math
import jax
import jax.numpy as jnp
import numpy as np
from jax import lax

D = 4096
HEADS = 32
HEAD_DIM = 128
SPAN = 64
LEVELS = 10
TOK_DEV = 512
TOKENS = 16384
WIDTH = 4096
NCHUNKS = 256
N_SEQ = 32
N_HEAD = 4


def shared_direction(key):
    return jax.random.truncated_normal(jax.random.fold_in(key, 101), -4.0, 4.0, (WIDTH,), jnp.float32)


def draw_queries(key, part):
    amount = 0.6
    noise = jax.random.truncated_normal(jax.random.fold_in(key, 211), -5.0, 5.0, (TOKENS, WIDTH), jnp.float32)
    return jnp.clip(amount * shared_direction(key)[None, :] + noise, -6.0, 6.0).astype(jnp.bfloat16)


def draw_keys(key, part):
    amount = 0.6
    noise = jax.random.truncated_normal(jax.random.fold_in(key, 307), -5.0, 5.0, (TOKENS, WIDTH), jnp.float32)
    return jnp.clip(amount * shared_direction(key)[None, :] + noise, -6.0, 6.0).astype(jnp.bfloat16)


def draw_log_decay(key, part):
    keys_list = jax.random.split(key, 7)
    slow_share = 0.5
    slow = jax.random.uniform(keys_list[0], (HEADS, 1)) < slow_share
    slow_rate = jnp.exp(jax.random.uniform(keys_list[1], (HEADS, 1), jnp.float32, math.log(0.05), math.log(0.6))) / TOKENS
    fast_rate = jnp.exp(jax.random.uniform(keys_list[2], (HEADS, 1), jnp.float32, math.log(1.0 / 50.0), math.log(1.0 / 30.0)))
    forgetting_rate = jnp.where(slow, slow_rate, fast_rate)
    segment_scaling_factor = jnp.exp(jax.random.uniform(keys_list[3], (HEADS, TOKENS // TOK_DEV), jnp.float32, math.log(0.5), math.log(2.0)))
    segment_scaling_factor = jnp.repeat(segment_scaling_factor, TOK_DEV, axis=1)
    stochastic_shift = jax.random.uniform(keys_list[4], (HEADS, TOKENS), jnp.float32, 0.5, 1.5)
    spots = jax.random.randint(keys_list[5], (4,), 0, TOKENS)
    omitted_elements = jax.random.uniform(keys_list[6], (4, 1), jnp.float32, math.log(0.5), math.log(0.8))
    index_sequence = jnp.arange(TOKENS)[None, :] == spots[:, None]
    clustered_occurrences = jnp.sum(jnp.where(index_sequence, omitted_elements, 0.0), axis=0)
    return (-forgetting_rate * segment_scaling_factor * stochastic_shift + clustered_occurrences[None, :]).astype(jnp.float32)


def draw_doc_start(key, part):
    keys_list = jax.random.split(jax.random.fold_in(key, 17), 2)
    half_count = NCHUNKS // 2
    positions = jnp.arange(NCHUNKS, dtype=jnp.int32)
    random_starts = jax.random.randint(keys_list[0], (NCHUNKS,), 0, 8) == 0
    forced_spot = half_count + jax.random.randint(keys_list[1], (), 0, NCHUNKS - half_count)
    flagged = random_starts & (positions >= half_count) | (positions == forced_spot)
    return flagged.astype(jnp.int32)


def shard_levels(stream_key, extent, cuts, least, high):
    loudness = 1.0
    for position, blocks in cuts:
        heights = jax.random.uniform(jax.random.fold_in(jax.random.fold_in(stream_key, 6), position), (blocks,), jnp.float32, least / len(cuts), high / len(cuts))
        loudness = loudness * jnp.repeat(jnp.exp(heights), extent[position] // blocks).reshape((-1,) + (1,) * (len(extent) - 1 - position))
    return loudness


def centred(key, dims, scale, bound, shards=(), kind=jnp.bfloat16):
    drawn = jax.random.normal(key, dims, jnp.float32) * scale
    if len(shards) > 0:
        drawn = shard_levels(key, dims, shards, -0.22, 0.18) * drawn
    return jnp.clip(drawn, min=-bound, max=bound).astype(kind)


def setup_inputs(seed: int = 0) -> dict:
    key_of = jax.random.split(jax.random.key(seed), 10)
    return {
        "queries": draw_queries(jax.random.fold_in(key_of[9], 71), 0),
        "keys": draw_keys(jax.random.fold_in(key_of[9], 71), 0),
        "values": centred(key_of[2], (TOKENS, WIDTH), 1.0, 6.0, ((0, 32), (1, 4))),
        "log_decay": draw_log_decay(jax.random.fold_in(key_of[9], 71), 0),
        "beta": jnp.clip(jnp.exp(math.log(0.03) - 3.4011973 * jax.random.uniform(key_of[4], (HEADS, TOKENS), jnp.float32) ** shard_levels(key_of[4], (HEADS, TOKENS), ((0, 4), (1, 32)), -0.2, 0.2)), 0.001, 0.03),
        "level_weights": jnp.clip(jnp.exp(math.log(2.0) - 2.0794415 * jax.random.uniform(key_of[5], (LEVELS, HEADS, TOKENS), jnp.float32) ** shard_levels(key_of[5], (LEVELS, HEADS, TOKENS), ((1, 4), (2, 32)), -0.2, 0.2)), 0.25, 2.0),
        "doc_start": draw_doc_start(jax.random.fold_in(key_of[9], 71), 0),
        "norm_gain": jnp.clip(1.0 + 0.15 * jax.random.normal(key_of[7], (WIDTH,), jnp.float32), 0.25, 1.75),
        "out_weight": centred(key_of[8], (WIDTH, D), WIDTH ** -0.5, 0.09375, ((0, 4),)),
    }


HIGH = lax.Precision.HIGHEST

def normalize(vector):
    return vector / jnp.sqrt(lax.optimization_barrier(jnp.sum(vector * vector, axis=-1, keepdims=True)) + 1e-06)

def compose(first, second):
    first_t, first_s = first
    second_token, second_s = second
    new_t = jnp.einsum('...de,...ef->...df', second_token, first_t, precision=HIGH)
    new_s = jnp.einsum('...de,...ef->...df', second_token, first_s, precision=HIGH) + second_s
    return (new_t, new_s)

def unit_lower_inverse(lower_part):
    span_len = lower_part.shape[-1]
    identity_span = jnp.eye(span_len, dtype=jnp.float32)
    power = -lower_part
    inverse = identity_span + power
    reach = 2
    while reach < span_len:
        power = jnp.einsum('...ij,...jk->...ik', power, power, precision=HIGH)
        inverse = jnp.einsum('...ij,...jk->...ik', inverse, identity_span + power, precision=HIGH)
        reach = reach * 2
    return inverse

def span_terms(query_c, key_c, value_c, log_c, beta_c):
    span_len = query_c.shape[-2]
    head_dim = query_c.shape[-1]
    cum_log = jnp.cumsum(log_c, axis=-1)
    gamma = jnp.exp(cum_log)
    row_ids = lax.broadcasted_iota(jnp.int32, (span_len, span_len), 0)
    col_ids = lax.broadcasted_iota(jnp.int32, (span_len, span_len), 1)
    inclusive = row_ids >= col_ids
    exacting_mode = row_ids > col_ids
    spread = cum_log[..., :, None] - cum_log[..., None, :]
    ratio = jnp.where(inclusive, jnp.exp(jnp.where(inclusive, spread, 0.0)), 0.0)
    key_key = jnp.einsum('...id,...jd->...ij', key_c, key_c, precision=HIGH)
    lower_part = jnp.where(exacting_mode, beta_c[..., :, None] * ratio * key_key, 0.0)
    rhs = jnp.concatenate([beta_c[..., None] * value_c, (beta_c * gamma)[..., None] * key_c], axis=-1)
    solved = jnp.einsum('...ij,...jd->...id', unit_lower_inverse(lower_part), rhs, precision=HIGH)
    new_values = solved[..., :head_dim]
    erasers = solved[..., head_dim:]
    scores = ratio * jnp.einsum('...id,...jd->...ij', query_c, key_c, precision=HIGH)
    reader = gamma[..., None] * query_c - jnp.einsum('...ij,...jd->...id', scores, erasers, precision=HIGH)
    intra = jnp.einsum('...ij,...jd->...id', scores, new_values, precision=HIGH)
    tail_keys = jnp.exp(cum_log[..., -1:] - cum_log)[..., None] * key_c
    identity_mat = jnp.eye(head_dim, dtype=jnp.float32)
    trans = gamma[..., -1][..., None, None] * identity_mat - jnp.einsum('...jd,...je->...de', tail_keys, erasers, precision=HIGH)
    write = jnp.einsum('...jd,...je->...de', tail_keys, new_values, precision=HIGH)
    return (reader, intra, trans, write)

def prepare(query_b, key_b, value_b, log_b, beta_b, weight_b, flags):
    tokens = query_b.shape[0]
    heads = log_b.shape[0]
    head_dim = query_b.shape[1] // heads
    count = tokens // SPAN

    def split_rows(matrix):
        return matrix.astype(jnp.float32).reshape(count, SPAN, heads, head_dim).transpose(0, 2, 1, 3)
    query_c = normalize(split_rows(query_b))
    key_c = normalize(split_rows(key_b))
    value_c = split_rows(value_b)
    log_c = log_b.reshape(heads, count, SPAN).transpose(1, 0, 2)
    beta_c = beta_b.reshape(heads, count, SPAN).transpose(1, 0, 2)
    weight_c = weight_b.reshape(weight_b.shape[0], heads, count, SPAN).transpose(2, 0, 1, 3)
    reader, intra, trans, write = span_terms(query_c, key_c, value_c, log_c, beta_c)
    keep = (1 - flags).astype(jnp.float32)
    return (reader, intra, trans, write, keep, weight_c)

def scan_summary(trans, write, keep):
    heads = trans.shape[1]
    head_dim = trans.shape[2]
    start = (jnp.broadcast_to(jnp.eye(head_dim, dtype=jnp.float32), (heads, head_dim, head_dim)), jnp.zeros((heads, head_dim, head_dim), jnp.float32))

    def step(carry, item):
        trans_c, write_c, keep_c = item
        return (compose(carry, (keep_c * trans_c, write_c)), None)
    return lax.scan(step, start, (trans, write, keep))[0]

def level_states(block_idx, buckets, heads, head_dim, low_levels):
    carried = jnp.broadcast_to(jnp.eye(head_dim, dtype=jnp.float32), (heads, head_dim, head_dim))
    states = [jnp.zeros((heads, head_dim, head_dim), jnp.float32) for level in range(low_levels + 1)]
    for level_bit in range(len(buckets)):
        flagged_binary_digit = block_idx >> level_bit & 1 == 1
        bucket_t, bucket_s = buckets[level_bit]
        states.append(jnp.where(flagged_binary_digit, jnp.einsum('hde,hef->hdf', carried, bucket_s, precision=HIGH), 0.0))
        carried = jnp.where(flagged_binary_digit, jnp.einsum('hde,hef->hdf', carried, bucket_t, precision=HIGH), carried)
    return jnp.stack(states)

def read_levels(reader, intra, trans, write, keep, weight_c, states):
    used = states.shape[0]
    count = reader.shape[0]
    merge_top = np.array([(i + 1 & -(i + 1)).bit_length() - 1 for i in range(count)], dtype=np.int32)
    slots = jnp.arange(used, dtype=jnp.int32)

    def step(carry, item):
        reader_c, intra_c, trans_c, write_c, keep_c, weight_now, top = item
        entering = keep_c * carry
        reads = jnp.einsum('hcd,lhde->lhce', reader_c, entering, precision=HIGH)
        weights = weight_now[:used]
        output = lax.optimization_barrier(jnp.sum(weights[..., None] * reads, axis=0)) + weights[0][..., None] * intra_c
        leaving = jnp.einsum('hde,lhef->lhdf', trans_c, entering, precision=HIGH)
        leaving = leaving.at[0].add(write_c)
        low = (slots <= top)[:, None, None, None]
        combined_levels = lax.optimization_barrier(jnp.sum(jnp.where(low, leaving, 0.0), axis=0))
        target = (slots == top + 1)[:, None, None, None]
        leaving = jnp.where(low, 0.0, leaving) + jnp.where(target, combined_levels[None], 0.0)
        return (leaving, output)
    return lax.scan(step, states, (reader, intra, trans, write, keep, weight_c, jnp.asarray(merge_top)))[1]

def finish(outputs, norm_gain):
    count, heads, span_len, head_dim = outputs.shape
    rows = outputs.transpose(0, 2, 1, 3).reshape(count * span_len, heads, head_dim)
    scaled = rows / jnp.sqrt(lax.optimization_barrier(jnp.mean(rows * rows, axis=-1, keepdims=True)) + 1e-06)
    scaled = scaled * norm_gain.reshape(heads, head_dim)
    return scaled.reshape(count * span_len, heads * head_dim).astype(jnp.bfloat16)

def reference(queries, keys, values, log_decay, beta, level_weights, doc_start, norm_gain, out_weight):
    nbits = N_SEQ.bit_length() - 1
    per_block = TOK_DEV // SPAN
    low_levels = per_block.bit_length() - 1

    def block_terms(block_idx):
        start = block_idx * TOK_DEV
        query_b = lax.dynamic_slice_in_dim(queries, start, TOK_DEV, 0)
        key_b = lax.dynamic_slice_in_dim(keys, start, TOK_DEV, 0)
        value_b = lax.dynamic_slice_in_dim(values, start, TOK_DEV, 0)
        log_b = lax.dynamic_slice_in_dim(log_decay, start, TOK_DEV, 1)
        beta_b = lax.dynamic_slice_in_dim(beta, start, TOK_DEV, 1)
        weight_b = lax.dynamic_slice_in_dim(level_weights, start, TOK_DEV, 2)
        flags = lax.dynamic_slice_in_dim(doc_start, block_idx * per_block, per_block, 0)
        return prepare(query_b, key_b, value_b, log_b, beta_b, weight_b, flags)

    def block_summary(block_idx):
        reader, intra, trans, write, keep, weight_c = block_terms(block_idx)
        return scan_summary(trans, write, keep)
    block_ids = jnp.arange(N_SEQ, dtype=jnp.int32)
    summaries = lax.map(block_summary, block_ids)
    tree = [summaries]
    for level_bit in range(nbits - 1):
        level_t, level_s = tree[-1]
        tree.append(compose((level_t[0::2], level_s[0::2]), (level_t[1::2], level_s[1::2])))
    group_width = WIDTH // N_HEAD

    def block_out(block_idx):
        reader, intra, trans, write, keep, weight_c = block_terms(block_idx)
        buckets = []
        for level_bit in range(nbits):
            sibling = jnp.bitwise_xor(block_idx >> level_bit, 1)
            buckets.append((tree[level_bit][0][sibling], tree[level_bit][1][sibling]))
        states = level_states(block_idx, buckets, HEADS, HEAD_DIM, low_levels)
        outputs = read_levels(reader, intra, trans, write, keep, weight_c, states)
        normed = finish(outputs, norm_gain)
        total = jnp.zeros((TOK_DEV, D), jnp.float32)
        for group in range(N_HEAD):
            partial_value = jnp.dot(normed[:, group * group_width:(group + 1) * group_width], out_weight[group * group_width:(group + 1) * group_width], preferred_element_type=jnp.float32).astype(jnp.bfloat16)
            partial_value = lax.optimization_barrier(partial_value)
            total = total + partial_value.astype(jnp.float32)
        return total.astype(jnp.bfloat16)
    return lax.map(block_out, block_ids).reshape(TOKENS, D)
```

```python
import functools

import jax
import jax.numpy as jnp
from jax import lax
from jax.experimental import pallas as pl
from jax.experimental.pallas import tpu as pltpu
from jax.sharding import PartitionSpec as P

SPAN = 64
SUPER = 128
HEAD_DIM = 128
LOCAL_LEVELS = 4
F32 = jnp.float32
BF16 = jnp.bfloat16


def mm(a, b):
    return jnp.dot(a, b, preferred_element_type=F32)


def mm_t(a, b):
    return lax.dot_general(a, b, (((1,), (1,)), ((), ())), preferred_element_type=F32)


def local_kernel(flags, q_ref, k_ref, v_ref, log_ref, beta_ref, weight_ref,
                 near_ref, far_ref, map_ref, cols_ref, rows_ref):
    head = pl.program_id(0)
    tokens = q_ref.shape[0]
    heads = log_ref.shape[0]
    supers = tokens // SUPER
    spans = tokens // SPAN
    row_i = lax.broadcasted_iota(jnp.int32, (SUPER, SUPER), 0)
    col_i = lax.broadcasted_iota(jnp.int32, (SUPER, SUPER), 1)
    same = (row_i // SPAN) == (col_i // SPAN)
    lower = same & (row_i >= col_i)
    strict = same & (row_i > col_i)
    eye = (row_i == col_i).astype(F32)

    @pl.when(head == 0)
    def _():
        upto = (same & (row_i <= col_i)).astype(F32)
        after = strict.astype(F32)
        both = jnp.concatenate([upto, after], axis=1)
        pieces = [
            jnp.dot(log_ref[:, s * SUPER:(s + 1) * SUPER], both,
                    precision=lax.Precision.HIGHEST, preferred_element_type=F32)
            for s in range(supers)
        ]
        cum = jnp.concatenate([p[:, :SUPER] for p in pieces], axis=1)
        tail = jnp.concatenate([p[:, SUPER:] for p in pieces], axis=1)
        span_i = lax.broadcasted_iota(jnp.int32, (heads, tokens), 1) // SPAN
        keep = jnp.ones((heads, tokens), F32)
        for j in range(spans):
            keep = jnp.where(span_i == j, (1 - flags[j]).astype(F32), keep)
        decay = jnp.exp(cum) * keep
        rows_ref[0] = cum
        rows_ref[1] = jnp.exp(tail)
        rows_ref[2] = decay
        rows_ref[3] = beta_ref[...] * decay
        rows_ref[4] = beta_ref[...]

    def row(i):
        return rows_ref[i, pl.ds(head, 1), :]

    wanted = [row(i) for i in range(5)]
    wanted += [weight_ref[level, pl.ds(head, 1), :] for level in range(9)]
    wanted += [jnp.zeros((2, tokens), F32)]
    cols = jnp.transpose(jnp.concatenate(wanted, axis=0))
    cols_ref[...] = cols

    cum_row = row(0)
    tail_row = row(1)

    readers, outs, maps = [], [], []
    for s in range(supers):
        t0 = s * SUPER
        c = cols[t0:t0 + SUPER, :]
        cum_c, decay_c, bdecay_c, beta_c, w0_c = (c[:, i:i + 1] for i in (0, 2, 3, 4, 5))
        qf = q_ref[t0:t0 + SUPER, :].astype(F32)
        kf = k_ref[t0:t0 + SUPER, :].astype(F32)
        vf = v_ref[t0:t0 + SUPER, :].astype(F32)
        qn = qf * lax.rsqrt(jnp.sum(qf * qf, axis=1, keepdims=True) + 1e-06)
        kn = kf * lax.rsqrt(jnp.sum(kf * kf, axis=1, keepdims=True) + 1e-06)
        qb = qn.astype(BF16)
        kb = kn.astype(BF16)
        k_t = jnp.transpose(kn)
        grams = mm_t(jnp.concatenate([qb, kb], axis=0), kb)
        ratio = jnp.exp(jnp.where(lower, cum_c - cum_row[:, t0:t0 + SUPER], -jnp.inf))
        scores = (ratio * grams[:SUPER]).astype(BF16)
        power = jnp.where(strict, -(beta_c * ratio) * grams[SUPER:], 0.0)
        inverse = eye + power
        pb = power.astype(BF16)
        pb = mm(pb, pb).astype(BF16)
        for step in range(4):
            both = mm(pb, jnp.concatenate([pb, inverse.astype(BF16)], axis=1))
            pb = both[:, :SUPER].astype(BF16)
            inverse = inverse + both[:, SUPER:]
        inverse = inverse + mm(pb, inverse.astype(BF16))
        rhs = jnp.concatenate([beta_c * vf, bdecay_c * kn], axis=1).astype(BF16)
        solved = mm(inverse.astype(BF16), rhs).astype(BF16)
        read = mm(scores, solved)
        outs.append(w0_c * read[:, :HEAD_DIM])
        readers.append((decay_c * qn - read[:, HEAD_DIM:]).astype(BF16))
        tails = (k_t * tail_row[:, t0:t0 + SUPER]).astype(BF16)
        for half in range(SUPER // SPAN):
            a, b = half * SPAN, (half + 1) * SPAN
            summary = mm(tails[:, a:b], solved[a:b, :])
            last = decay_c[b - 1:b, :]
            maps.append((summary[:, :HEAD_DIM], eye * last - summary[:, HEAD_DIM:]))

    outs = [o[a:a + SPAN] for o in outs for a in range(0, SUPER, SPAN)]
    readers = [r[a:a + SPAN] for r in readers for a in range(0, SUPER, SPAN)]
    for level in range(1, LOCAL_LEVELS):
        new_outs, new_readers, new_maps = [], [], []
        for i in range(0, len(maps), 2):
            (s_lo, t_lo), (s_hi, t_hi) = maps[i], maps[i + 1]
            r_hi = readers[i + 1]
            n = r_hi.shape[0]
            t0 = (i + 1) * n
            w_c = cols[t0:t0 + n, 5 + level:6 + level]
            both = mm(jnp.concatenate([r_hi, t_hi.astype(BF16)], axis=0),
                      jnp.concatenate([s_lo.astype(BF16), t_lo.astype(BF16)], axis=1))
            new_outs.append(jnp.concatenate([outs[i], outs[i + 1] + w_c * both[:n, :HEAD_DIM]], axis=0))
            new_readers.append(jnp.concatenate([readers[i], both[:n, HEAD_DIM:].astype(BF16)], axis=0))
            new_maps.append((both[n:, :HEAD_DIM] + s_hi, both[n:, HEAD_DIM:]))
        outs, readers, maps = new_outs, new_readers, new_maps
    near_ref[...] = outs[0]
    far_ref[...] = readers[0]
    map_ref[0] = jnp.concatenate(maps[0], axis=1).astype(BF16)


def local_part(flags, queries, keys, values, log_decay, beta, weights):
    tokens, width = queries.shape
    heads = log_decay.shape[0]
    block = pl.BlockSpec((tokens, HEAD_DIM), lambda h, f: (0, h))
    whole2 = pl.BlockSpec((heads, tokens), lambda h, f: (0, 0))
    whole3 = pl.BlockSpec(weights.shape, lambda h, f: (0, 0, 0))
    return pl.pallas_call(
        local_kernel,
        grid_spec=pltpu.PrefetchScalarGridSpec(
            num_scalar_prefetch=1,
            grid=(heads,),
            in_specs=[block, block, block, whole2, whole2, whole3],
            out_specs=[block, block,
                       pl.BlockSpec((1, HEAD_DIM, 2 * HEAD_DIM), lambda h, f: (h, 0, 0)),
                       pl.BlockSpec((tokens, 16), lambda h, f: (h, 0))],
            scratch_shapes=[pltpu.VMEM((5, heads, tokens), F32)],
        ),
        out_shape=[
            jax.ShapeDtypeStruct((tokens, width), F32),
            jax.ShapeDtypeStruct((tokens, width), BF16),
            jax.ShapeDtypeStruct((heads, HEAD_DIM, 2 * HEAD_DIM), BF16),
            jax.ShapeDtypeStruct((heads * tokens, 16), F32),
        ],
        name="local_part",
    )(flags, queries, keys, values, log_decay, beta, weights)


def pair_kernel(bits, mine_ref, sib_ref, cur_ref):
    core = bits[0]
    half = cur_ref.shape[0]

    def run(first, second):
        for g in range(half):
            h = half * core + g
            later = second[h]
            both = mm(later[:, HEAD_DIM:], first[h])
            cur_ref[g, :, :HEAD_DIM] = (both[:, :HEAD_DIM] + later[:, :HEAD_DIM].astype(F32)).astype(BF16)
            cur_ref[g, :, HEAD_DIM:] = both[:, HEAD_DIM:].astype(BF16)

    @pl.when(core == 1)
    def _():
        run(sib_ref, mine_ref)

    @pl.when(core == 0)
    def _():
        run(mine_ref, sib_ref)


def level_kernel(level, bits, *refs):
    if level == 1:
        sib_ref, cur_ref, new_ref, x_ref, carry_ref = refs
    else:
        sib_ref, cur_ref, carried_ref, new_ref, x_ref, carry_ref = refs
    bit = bits[level]
    half = cur_ref.shape[0]

    def store(g, both, later):
        new_ref[g, :, :HEAD_DIM] = (both[:, :HEAD_DIM] + later[:, :HEAD_DIM].astype(F32)).astype(BF16)
        new_ref[g, :, HEAD_DIM:] = both[:, HEAD_DIM:].astype(BF16)

    @pl.when(bit == 1)
    def _():
        for g in range(half):
            later, sib = cur_ref[g], sib_ref[g]
            if level == 1:
                store(g, mm(later[:, HEAD_DIM:], sib), later)
                x_ref[g] = sib[:, :HEAD_DIM]
                carry_ref[g] = sib[:, HEAD_DIM:]
            else:
                both = mm(jnp.concatenate([later[:, HEAD_DIM:], carried_ref[g]], axis=0), sib)
                store(g, both[:HEAD_DIM], later)
                x_ref[g] = both[HEAD_DIM:, :HEAD_DIM].astype(BF16)
                carry_ref[g] = both[HEAD_DIM:, HEAD_DIM:].astype(BF16)

    @pl.when(bit == 0)
    def _():
        row_i = lax.broadcasted_iota(jnp.int32, (HEAD_DIM, HEAD_DIM), 0)
        col_i = lax.broadcasted_iota(jnp.int32, (HEAD_DIM, HEAD_DIM), 1)
        eye = (row_i == col_i).astype(F32).astype(BF16)
        for g in range(half):
            later = sib_ref[g]
            store(g, mm(later[:, HEAD_DIM:], cur_ref[g]), later)
            x_ref[g] = jnp.zeros((HEAD_DIM, HEAD_DIM), BF16)
            carry_ref[g] = eye if level == 1 else carried_ref[g]


def top_kernel(level, bits, sib_ref, carried_ref, x_ref):
    bit = bits[level]

    @pl.when(bit == 1)
    def _():
        for g in range(x_ref.shape[0]):
            x_ref[g] = mm(carried_ref[g], sib_ref[g]).astype(BF16)

    @pl.when(bit == 0)
    def _():
        x_ref[...] = jnp.zeros(x_ref.shape, BF16)


def small_call(kernel, bits, args, outs, name):
    spec = [pl.BlockSpec(a.shape, lambda i, b, n=a.ndim: (0,) * n) for a in args]
    flops = 2 * 256 * 128 * 256 * args[0].shape[0]
    return pl.pallas_call(
        kernel,
        grid_spec=pltpu.PrefetchScalarGridSpec(
            num_scalar_prefetch=1,
            grid=(1,),
            in_specs=spec,
            out_specs=[pl.BlockSpec(o.shape, lambda i, b, n=len(o.shape): (0,) * n) for o in outs],
        ),
        out_shape=outs,
        cost_estimate=pl.CostEstimate(flops=flops, bytes_accessed=1 << 20, transcendentals=0),
        name=name,
    )(bits, *args)


def final_kernel(bits, near_ref, far_ref, sib_ref, cols_ref, gain_ref, *refs):
    head = pl.program_id(0)
    core = bits[0]
    levels = (len(refs) - 1) // 2
    mine, other, z_ref = refs[:levels], refs[levels:2 * levels], refs[-1]
    half = pl.num_programs(0) // 2
    is_mine = (head // half) == core
    states = jnp.concatenate(
        [jnp.where(is_mine, m[0], o[0]) for m, o in zip(mine, other)], axis=1)
    first = 5 + LOCAL_LEVELS
    rows = 128
    for t0 in range(0, near_ref.shape[0], rows):
        cut = slice(t0, t0 + rows)
        far = far_ref[cut, :]
        both = mm(far, sib_ref[0])
        c = cols_ref[cut, :]
        y = near_ref[cut, :] + jnp.where(core == 1, c[:, first:first + 1], 0.0) * both[:, :HEAD_DIM]
        far = jnp.where(core == 1, both[:, HEAD_DIM:].astype(BF16), far)
        reads = mm(far, states)
        for i in range(levels):
            y = y + c[:, first + 1 + i:first + 2 + i] * reads[:, i * HEAD_DIM:(i + 1) * HEAD_DIM]
        scale = lax.rsqrt(jnp.mean(y * y, axis=1, keepdims=True) + 1e-06)
        z_ref[cut, :] = (y * scale * gain_ref[...]).astype(BF16)


def final_part(bits, near, far, sib, cols, gain, mine, other):
    tokens, width = near.shape
    heads = sib.shape[0]
    half = heads // 2
    block = pl.BlockSpec((tokens, HEAD_DIM), lambda h, b: (0, h))
    state = pl.BlockSpec((1, HEAD_DIM, HEAD_DIM), lambda h, b: (h % half, 0, 0))
    return pl.pallas_call(
        final_kernel,
        grid_spec=pltpu.PrefetchScalarGridSpec(
            num_scalar_prefetch=1,
            grid=(heads,),
            in_specs=[block, block,
                      pl.BlockSpec((1, HEAD_DIM, 2 * HEAD_DIM), lambda h, b: (h, 0, 0)),
                      pl.BlockSpec((tokens, 16), lambda h, b: (h, 0)),
                      pl.BlockSpec((1, HEAD_DIM), lambda h, b: (0, h))]
                     + [state] * (2 * len(mine)),
            out_specs=block,
        ),
        out_shape=jax.ShapeDtypeStruct((tokens, width), BF16),
        name="final_part",
    )(bits, near, far, sib, cols, gain.reshape(1, width), *mine, *other)


def partner(value, bit):
    size = lax.axis_size("seq")
    return lax.ppermute(value, "seq", [(i, i ^ (1 << bit)) for i in range(size)])


def project(z, out_weight):
    size = lax.axis_size("head")
    me = lax.axis_index("head")
    rows = z.shape[0] // size
    cols = out_weight.shape[1] // 2
    up = [(j, (j + 1) % size) for j in range(size)]
    down = [(j, (j - 1) % size) for j in range(size)]

    def term(block, side):
        part = lax.dynamic_slice_in_dim(z, (block % size) * rows, rows, 0)
        w = out_weight[:, side * cols:(side + 1) * cols]
        return jnp.dot(part, w, preferred_element_type=F32).astype(BF16)

    a = term(me + size - 1, 0)
    b = term(me + 1, 1)
    for s in range(size - 1):
        got_a = lax.ppermute(a, "head", up)
        got_b = lax.ppermute(b, "head", down)
        own_a = lax.optimization_barrier(term(me + 2 * size - 2 - s, 0))
        own_b = lax.optimization_barrier(term(me + 2 + s, 1))
        a = (got_a.astype(F32) + own_a.astype(F32)).astype(BF16)
        b = (got_b.astype(F32) + own_b.astype(F32)).astype(BF16)
    return jnp.concatenate([a, b], axis=1)


def body(queries, keys, values, log_decay, beta, level_weights, doc_start, norm_gain, out_weight):
    heads = log_decay.shape[0]
    half = heads // 2
    nbits = lax.axis_size("seq").bit_length() - 1
    index = lax.axis_index("seq")
    bits = jnp.stack([(index >> b) & 1 for b in range(nbits)]).astype(jnp.int32)
    near, far, mine, cols = local_part(doc_start, queries, keys, values, log_decay, beta, level_weights)
    sib0 = partner(mine, 0)
    wide = jax.ShapeDtypeStruct((half, HEAD_DIM, 2 * HEAD_DIM), BF16)
    square = jax.ShapeDtypeStruct((half, HEAD_DIM, HEAD_DIM), BF16)
    cur = small_call(pair_kernel, bits, [mine, sib0], [wide], "pair")[0]
    carried = None
    states, others = [], []
    for level in range(1, nbits):
        if level < nbits - 1:
            sib = partner(cur, level)
            args = [sib, cur] if level == 1 else [sib, cur, carried]
            cur, x, carried = small_call(
                functools.partial(level_kernel, level), bits, args, [wide, square, square], f"level{level}")
        else:
            sib = partner(cur[:, :, :HEAD_DIM], level)
            x = small_call(functools.partial(top_kernel, level), bits, [sib, carried], [square], "top")[0]
        states.append(x)
        others.append(partner(x, 0))
    z = final_part(bits, near, far, sib0, cols, norm_gain, states, others)
    return project(z, out_weight)


def solution(mesh):
    placed = (
        P("seq", "head"),
        P("seq", "head"),
        P("seq", "head"),
        P("head", "seq"),
        P("head", "seq"),
        P(None, "head", "seq"),
        P("seq"),
        P("head"),
        P("head", None),
    )
    return jax.shard_map(
        body, mesh=mesh, in_specs=placed, out_specs=P(("seq", "head"), None), check_vma=False
    )
```

```python
import functools
import jax
import jax.numpy as jnp
from jax import lax
from jax.experimental import pallas as pl
from jax.experimental.pallas import tpu as pltpu
from jax.sharding import PartitionSpec as P

SPAN = 64
SUPER = 128
HEAD_DIM = 128
LOCAL_LEVELS = 4
TOGETHER = 2
CHUNKS = 2
PIECES = 2
EPS = 1e-06
F32 = jnp.float32
BF16 = jnp.bfloat16


def mm(a, b):
    return jnp.dot(a, b, preferred_element_type=F32)


def local_kernel(chunk, flags, q_ref, k_ref, v_ref, log_ref, beta_ref, weight_ref,
                 near_ref, far_ref, map_ref, cols_ref, rows_ref):
    step = pl.program_id(0)
    tokens = q_ref.shape[0]
    heads = log_ref.shape[0]
    supers = tokens // SUPER
    spans = tokens // SPAN
    row_i = lax.broadcasted_iota(jnp.int32, (SUPER, SUPER), 0)
    col_i = lax.broadcasted_iota(jnp.int32, (SUPER, SUPER), 1)
    same = (row_i >> 6) == (col_i >> 6)
    lower = same & (row_i >= col_i)
    strict = same & (row_i > col_i)
    eye = (row_i == col_i).astype(F32)

    @pl.when(step == 0)
    def _():
        upto = (same & (row_i <= col_i)).astype(F32)
        both = jnp.concatenate([upto, strict.astype(F32)], axis=1)
        pieces = [
            jnp.dot(log_ref[:, s * SUPER:(s + 1) * SUPER], both,
                    precision=lax.Precision.HIGHEST, preferred_element_type=F32)
            for s in range(supers)
        ]
        cum = jnp.concatenate([p[:, :SUPER] for p in pieces], axis=1)
        tail = jnp.concatenate([p[:, SUPER:] for p in pieces], axis=1)
        span_i = lax.broadcasted_iota(jnp.int32, (heads, tokens), 1) >> 6
        keep = jnp.ones((heads, tokens), F32)
        for j in range(spans):
            keep = jnp.where(span_i == j, (1 - flags[j]).astype(F32), keep)
        rows_ref[0] = cum
        rows_ref[1] = jnp.exp(tail)
        rows_ref[2] = jnp.exp(cum) * keep

    units = [(g, s) for g in range(TOGETHER) for s in range(supers)]
    cols, cum_rows, tail_rows, beta_rows = [], [], [], []
    for g in range(TOGETHER):
        head = TOGETHER * (CHUNKS * step + chunk) + g
        take = pl.ds(head, 1)
        beta_row = beta_ref[take, :]
        wanted = [rows_ref[0, take, :], rows_ref[2, take, :], beta_row]
        wanted += [weight_ref[level, take, :] for level in range(9)]
        wanted += [jnp.zeros((4, tokens), F32)]
        c = jnp.transpose(jnp.concatenate(wanted, axis=0))
        cols_ref[g * tokens:(g + 1) * tokens, :] = c
        cols.append(c)
        cum_rows.append(rows_ref[0, take, :])
        tail_rows.append(rows_ref[1, take, :])
        beta_rows.append(beta_row)

    def cut(s):
        return slice(s * SUPER, (s + 1) * SUPER)

    def lanes(g):
        return slice(g * HEAD_DIM, (g + 1) * HEAD_DIM)

    def col(g, s, i):
        return cols[g][cut(s), i:i + 1]

    scores, powers, inverses, right, tails, queries = [], [], [], [], [], []
    for g, s in units:
        q = q_ref[cut(s), lanes(g)]
        k = k_ref[cut(s), lanes(g)]
        k_t = jnp.transpose(k)
        grams = mm(jnp.concatenate([q, k], axis=0), k_t)
        qf, kf, ktf = q.astype(F32), k.astype(F32), k_t.astype(F32)
        rq = lax.rsqrt(jnp.sum(qf * qf, axis=1, keepdims=True) + EPS)
        rk = lax.rsqrt(jnp.sum(kf * kf, axis=1, keepdims=True) + EPS)
        rk_row = lax.rsqrt(jnp.sum(ktf * ktf, axis=0, keepdims=True) + EPS)
        spread = col(g, s, 0) - cum_rows[g][:, cut(s)]
        ratio = jnp.exp(jnp.where(lower, spread, -1e30)) * rk_row
        scores.append((ratio * (rq * grams[:SUPER])).astype(BF16))
        power = jnp.where(strict, (-col(g, s, 2) * rk) * ratio * grams[SUPER:], 0.0)
        inverses.append(eye + power)
        powers.append(power.astype(BF16))
        decay = col(g, s, 1)
        right.append(jnp.concatenate([v_ref[cut(s), lanes(g)], (decay * rk * kf).astype(BF16)], axis=1))
        tails.append((ktf * (rk_row * tail_rows[g][:, cut(s)])).astype(BF16))
        queries.append(decay * rq * qf)

    n = len(units)
    powers = [mm(p, p).astype(BF16) for p in powers]
    for _ in range(4):
        both = [mm(powers[u], jnp.concatenate([powers[u], inverses[u].astype(BF16)], axis=1)) for u in range(n)]
        powers = [b[:, :SUPER].astype(BF16) for b in both]
        inverses = [inverses[u] + both[u][:, SUPER:] for u in range(n)]
    inverses = [inverses[u] + mm(powers[u], inverses[u].astype(BF16)) for u in range(n)]
    solved = []
    for u, (g, s) in enumerate(units):
        scaled = (inverses[u] * beta_rows[g][:, cut(s)]).astype(BF16)
        solved.append(mm(scaled, right[u]).astype(BF16))
    leaves = [[] for _ in range(TOGETHER)]
    for u, (g, s) in enumerate(units):
        for half in range(SUPER // SPAN):
            a, b = half * SPAN, (half + 1) * SPAN
            summary = mm(tails[u][:, a:b], solved[u][a:b, :])
            t = s * SUPER + b - 1
            last = jnp.broadcast_to(cols[g][t:t + 1, 1:2], (1, HEAD_DIM))
            leaves[g].append((summary[:, :HEAD_DIM], summary[:, HEAD_DIM:], last))
    outs = [[] for _ in range(TOGETHER)]
    readers = [[] for _ in range(TOGETHER)]
    for u, (g, s) in enumerate(units):
        read = mm(scores[u], solved[u])
        out = col(g, s, 3) * read[:, :HEAD_DIM]
        reader = queries[u] - read[:, HEAD_DIM:]
        for half in range(SUPER // SPAN):
            a, b = half * SPAN, (half + 1) * SPAN
            outs[g].append(out[a:b])
            readers[g].append(reader[a:b])

    for level in range(1, LOCAL_LEVELS):
        for g in range(TOGETHER):
            maps = leaves[g]
            new_outs, new_readers, new_maps = [], [], []
            for i in range(0, len(maps), 2):
                (s_lo, e_lo, d_lo), (s_hi, e_hi, d_hi) = maps[i], maps[i + 1]
                r_hi = readers[g][i + 1]
                m = r_hi.shape[0]
                t0 = (i + 1) * m
                w_c = cols[g][t0:t0 + m, 3 + level:4 + level]
                both = mm(jnp.concatenate([r_hi.astype(BF16), e_hi.astype(BF16)], axis=0),
                          jnp.concatenate([s_lo.astype(BF16), e_lo.astype(BF16)], axis=1))
                new_outs.append(jnp.concatenate(
                    [outs[g][i], outs[g][i + 1] + w_c * both[:m, :HEAD_DIM]], axis=0))
                new_readers.append(jnp.concatenate(
                    [readers[g][i], d_lo * r_hi - both[:m, HEAD_DIM:]], axis=0))
                new_maps.append((d_hi * s_lo + s_hi - both[m:, :HEAD_DIM],
                                 d_hi * e_lo + d_lo * e_hi - both[m:, HEAD_DIM:],
                                 d_lo * d_hi))
            outs[g], readers[g], leaves[g] = new_outs, new_readers, new_maps
    for g in range(TOGETHER):
        total, erase, decay = leaves[g][0]
        near_ref[:, lanes(g)] = outs[g][0]
        far_ref[:, lanes(g)] = readers[g][0].astype(BF16)
        map_ref[g] = jnp.concatenate([total, eye * decay - erase], axis=1).astype(BF16)


def local_part(chunk, flags, queries, keys, values, log_decay, beta, weights):
    tokens, width = queries.shape
    heads = log_decay.shape[0]
    steps = heads // (TOGETHER * CHUNKS)
    wide = TOGETHER * HEAD_DIM
    block = pl.BlockSpec((tokens, wide), lambda h, f: (0, CHUNKS * h + chunk))
    out = pl.BlockSpec((tokens, wide), lambda h, f: (0, h))
    whole2 = pl.BlockSpec((heads, tokens), lambda h, f: (0, 0))
    whole3 = pl.BlockSpec(weights.shape, lambda h, f: (0, 0, 0))
    part = steps * TOGETHER
    return pl.pallas_call(
        functools.partial(local_kernel, chunk),
        grid_spec=pltpu.PrefetchScalarGridSpec(
            num_scalar_prefetch=1,
            grid=(steps,),
            in_specs=[block, block, block, whole2, whole2, whole3],
            out_specs=[out, out,
                       pl.BlockSpec((TOGETHER, HEAD_DIM, 2 * HEAD_DIM), lambda h, f: (h, 0, 0)),
                       pl.BlockSpec((TOGETHER * tokens, 16), lambda h, f: (h, 0))],
            scratch_shapes=[pltpu.VMEM((3, heads, tokens), F32)],
        ),
        out_shape=[
            jax.ShapeDtypeStruct((tokens, part * HEAD_DIM), F32),
            jax.ShapeDtypeStruct((tokens, part * HEAD_DIM), BF16),
            jax.ShapeDtypeStruct((part, HEAD_DIM, 2 * HEAD_DIM), BF16),
            jax.ShapeDtypeStruct((part * tokens, 16), F32),
        ],
        compiler_params=pltpu.CompilerParams(vmem_limit_bytes=24 << 20),
        cost_estimate=pl.CostEstimate(flops=part * 1500000000, bytes_accessed=8 << 20, transcendentals=0),
        name=f"local{chunk}",
    )(flags, queries, keys, values, log_decay, beta, weights)


def pair_kernel(bits, mine_ref, sib_ref, cur_ref):
    core = bits[0]
    half = cur_ref.shape[0]

    def run(first, second):
        for g in range(half):
            later = second[half * core + g]
            both = mm(later[:, HEAD_DIM:], first[half * core + g])
            cur_ref[g, :, :HEAD_DIM] = (both[:, :HEAD_DIM] + later[:, :HEAD_DIM].astype(F32)).astype(BF16)
            cur_ref[g, :, HEAD_DIM:] = both[:, HEAD_DIM:].astype(BF16)

    @pl.when(core == 1)
    def _():
        run(sib_ref, mine_ref)

    @pl.when(core == 0)
    def _():
        run(mine_ref, sib_ref)


def level_kernel(level, bits, *refs):
    if level == 1:
        sib_ref, cur_ref, new_ref, x_ref, carry_ref = refs
    else:
        sib_ref, cur_ref, carried_ref, new_ref, x_ref, carry_ref = refs
    bit = bits[level]
    half = cur_ref.shape[0]

    def store(g, both, later):
        new_ref[g, :, :HEAD_DIM] = (both[:, :HEAD_DIM] + later[:, :HEAD_DIM].astype(F32)).astype(BF16)
        new_ref[g, :, HEAD_DIM:] = both[:, HEAD_DIM:].astype(BF16)

    @pl.when(bit == 1)
    def _():
        for g in range(half):
            later, sib = cur_ref[g], sib_ref[g]
            if level == 1:
                store(g, mm(later[:, HEAD_DIM:], sib), later)
                x_ref[g] = sib[:, :HEAD_DIM]
                carry_ref[g] = sib[:, HEAD_DIM:]
            else:
                both = mm(jnp.concatenate([later[:, HEAD_DIM:], carried_ref[g]], axis=0), sib)
                store(g, both[:HEAD_DIM], later)
                x_ref[g] = both[HEAD_DIM:, :HEAD_DIM].astype(BF16)
                carry_ref[g] = both[HEAD_DIM:, HEAD_DIM:].astype(BF16)

    @pl.when(bit == 0)
    def _():
        row_i = lax.broadcasted_iota(jnp.int32, (HEAD_DIM, HEAD_DIM), 0)
        col_i = lax.broadcasted_iota(jnp.int32, (HEAD_DIM, HEAD_DIM), 1)
        eye = (row_i == col_i).astype(F32).astype(BF16)
        for g in range(half):
            later = sib_ref[g]
            store(g, mm(later[:, HEAD_DIM:], cur_ref[g]), later)
            x_ref[g] = jnp.zeros((HEAD_DIM, HEAD_DIM), BF16)
            carry_ref[g] = eye if level == 1 else carried_ref[g]


def top_kernel(level, bits, sib_ref, carried_ref, x_ref):
    bit = bits[level]

    @pl.when(bit == 1)
    def _():
        for g in range(x_ref.shape[0]):
            x_ref[g] = mm(carried_ref[g], sib_ref[g]).astype(BF16)

    @pl.when(bit == 0)
    def _():
        x_ref[...] = jnp.zeros(x_ref.shape, BF16)


def small_call(kernel, bits, args, outs, name):
    return pl.pallas_call(
        kernel,
        grid_spec=pltpu.PrefetchScalarGridSpec(
            num_scalar_prefetch=1,
            grid=(1,),
            in_specs=[pl.BlockSpec(a.shape, lambda i, b, n=a.ndim: (0,) * n) for a in args],
            out_specs=[pl.BlockSpec(o.shape, lambda i, b, n=len(o.shape): (0,) * n) for o in outs],
        ),
        out_shape=outs,
        compiler_params=pltpu.CompilerParams(vmem_limit_bytes=6 << 20),
        cost_estimate=pl.CostEstimate(flops=600000000, bytes_accessed=1 << 20, transcendentals=0),
        name=name,
    )(bits, *args)


def final_kernel(levels, bits, near_ref, far_ref, sib_ref, cols_ref, gain_ref, *refs):
    core = bits[0]
    mine, other, z_ref = refs[:levels], refs[levels:2 * levels], refs[-1]
    tokens = near_ref.shape[0]
    is_mine = pl.program_id(0) == core
    first = 3 + LOCAL_LEVELS
    upper = core == 1
    units = [(g, t) for g in range(TOGETHER) for t in range(0, tokens, SUPER)]
    states = [jnp.concatenate([jnp.where(is_mine, m[g], o[g]) for m, o in zip(mine, other)], axis=1)
              for g in range(TOGETHER)]

    def lanes(g):
        return slice(g * HEAD_DIM, (g + 1) * HEAD_DIM)

    def cols(g, t, i):
        return cols_ref[g * tokens + t:g * tokens + t + SUPER, i:i + 1]

    fars = [far_ref[t:t + SUPER, lanes(g)] for g, t in units]
    both = [mm(fars[u], sib_ref[g]) for u, (g, t) in enumerate(units)]
    ys = [near_ref[t:t + SUPER, lanes(g)]
          + jnp.where(upper, cols(g, t, first), 0.0) * both[u][:, :HEAD_DIM] for u, (g, t) in enumerate(units)]
    fars = [jnp.where(upper, both[u][:, HEAD_DIM:].astype(BF16), fars[u]) for u in range(len(units))]
    for u, (g, t) in enumerate(units):
        reads = mm(fars[u], states[g])
        y = ys[u]
        for i in range(levels):
            y = y + cols(g, t, first + 1 + i) * reads[:, i * HEAD_DIM:(i + 1) * HEAD_DIM]
        scale = lax.rsqrt(jnp.mean(y * y, axis=1, keepdims=True) + EPS)
        z_ref[t:t + SUPER, lanes(g)] = (y * scale * gain_ref[:, lanes(g)]).astype(BF16)


def final_part(chunk, bits, near, far, sib, cols, gain, mine, other, before):
    tokens, width = near.shape
    wide = TOGETHER * HEAD_DIM
    steps = width // wide
    levels = len(mine)
    block = pl.BlockSpec((tokens, wide), lambda h, b: (0, h))
    placed = lambda h, b: (0, CHUNKS * h + chunk)
    state = pl.BlockSpec((TOGETHER, HEAD_DIM, HEAD_DIM), lambda h, b: (0, 0, 0))
    in_specs = [block, block,
                pl.BlockSpec((TOGETHER, HEAD_DIM, 2 * HEAD_DIM), lambda h, b: (h, 0, 0)),
                pl.BlockSpec((TOGETHER * tokens, 16), lambda h, b: (h, 0)),
                pl.BlockSpec((1, wide), placed)] + [state] * (2 * levels)
    args = [bits, near, far, sib, cols, gain, *mine, *other]
    aliases = {}
    if before is not None:
        aliases = {len(args): 0}
        args.append(before)
        in_specs.append(pl.BlockSpec(memory_space=pl.ANY))
    return pl.pallas_call(
        functools.partial(final_kernel, levels),
        grid_spec=pltpu.PrefetchScalarGridSpec(
            num_scalar_prefetch=1,
            grid=(steps,),
            in_specs=in_specs,
            out_specs=pl.BlockSpec((tokens, wide), placed),
        ),
        out_shape=jax.ShapeDtypeStruct((tokens, CHUNKS * width), BF16),
        input_output_aliases=aliases,
        compiler_params=pltpu.CompilerParams(vmem_limit_bytes=20 << 20),
        cost_estimate=pl.CostEstimate(flops=3000000000, bytes_accessed=8 << 20, transcendentals=0),
        name=f"final{chunk}",
    )(*args)


def partner(value, bit):
    size = lax.axis_size("seq")
    return lax.ppermute(value, "seq", [(i, i ^ (1 << bit)) for i in range(size)])


def project(z, out_weight):
    size = lax.axis_size("head")
    me = lax.axis_index("head")
    rows = z.shape[0] // size
    cols = out_weight.shape[1] // (2 * PIECES)
    up = [(j, (j + 1) % size) for j in range(size)]
    down = [(j, (j - 1) % size) for j in range(size)]

    def term(block, piece):
        part = lax.dynamic_slice_in_dim(z, (block % size) * rows, rows, 0)
        w = out_weight[:, piece * cols:(piece + 1) * cols]
        return jnp.dot(part, w, preferred_element_type=F32).astype(BF16)

    order = [p for i in range(PIECES) for p in (i, PIECES + i)]
    sums = {p: term(me + size - 1 if p < PIECES else me + 1, p) for p in order}
    for s in range(size - 1):
        got = {p: lax.ppermute(sums[p], "head", up if p < PIECES else down) for p in order}
        own = {p: lax.optimization_barrier(
            term(me + 2 * size - 2 - s if p < PIECES else me + 2 + s, p)) for p in order}
        sums = {p: (got[p].astype(F32) + own[p].astype(F32)).astype(BF16) for p in order}
    return jnp.concatenate([sums[p] for p in range(2 * PIECES)], axis=1)


def body(queries, keys, values, log_decay, beta, level_weights, doc_start, norm_gain, out_weight):
    heads = log_decay.shape[0]
    mine_heads = heads // (2 * CHUNKS)
    nbits = lax.axis_size("seq").bit_length() - 1
    index = lax.axis_index("seq")
    bits = jnp.stack([(index >> b) & 1 for b in range(nbits)]).astype(jnp.int32)
    gain = norm_gain.reshape(1, -1)
    wide = jax.ShapeDtypeStruct((mine_heads, HEAD_DIM, 2 * HEAD_DIM), BF16)
    square = jax.ShapeDtypeStruct((mine_heads, HEAD_DIM, HEAD_DIM), BF16)
    local, sibs, curs = [], [], []
    for chunk in range(CHUNKS):
        local.append(local_part(chunk, doc_start, queries, keys, values, log_decay, beta, level_weights))
        mine = local[chunk][2]
        sibs.append(partner(mine, 0))
        curs.append(small_call(pair_kernel, bits, [mine, sibs[chunk]], [wide], f"pair{chunk}")[0])
    carried = [None] * CHUNKS
    states = [[] for _ in range(CHUNKS)]
    others = [[] for _ in range(CHUNKS)]
    for level in range(1, nbits):
        for c in range(CHUNKS):
            if level < nbits - 1:
                sib = partner(curs[c], level)
                args = [sib, curs[c]] if level == 1 else [sib, curs[c], carried[c]]
                curs[c], x, carried[c] = small_call(
                    functools.partial(level_kernel, level), bits, args, [wide, square, square],
                    f"level{level}{c}")
            else:
                sib = partner(curs[c][:, :, :HEAD_DIM], level)
                x = small_call(functools.partial(top_kernel, level), bits, [sib, carried[c]], [square],
                               f"top{c}")[0]
            states[c].append(x)
            others[c].append(partner(x, 0))
    z = None
    for c in range(CHUNKS):
        near, far, _, cols = local[c]
        z = final_part(c, bits, near, far, sibs[c], cols, gain, states[c], others[c], z)
    return project(z, out_weight)


def solution(mesh):
    placed = (
        P("seq", "head"),
        P("seq", "head"),
        P("seq", "head"),
        P("head", "seq"),
        P("head", "seq"),
        P(None, "head", "seq"),
        P("seq"),
        P("head"),
        P("head", None),
    )
    return jax.shard_map(
        body, mesh=mesh, in_specs=placed, out_specs=P(("seq", "head"), None), check_vma=False
    )
```

```python
import functools
import jax
import jax.numpy as jnp
from jax import lax
from jax.experimental import pallas as pl
from jax.experimental.pallas import tpu as pltpu
from jax.sharding import PartitionSpec as P


SPAN = 64
SUPER = 128
HEAD_DIM = 128
LOCAL_LEVELS = 4
TOGETHER = 2
CHUNKS = 2
PIECES = 2
EPS = 1e-06
F32 = jnp.float32
BF16 = jnp.bfloat16


def mm(a, b):
    return jnp.dot(a, b, preferred_element_type=F32)


def local_kernel(base, stride, flags, q_ref, k_ref, v_ref, log_ref, beta_ref, weight_ref,
                 near_ref, far_ref, map_ref, cols_ref, rows_ref):
    step = pl.program_id(0)
    tokens = q_ref.shape[0]
    heads = log_ref.shape[0]
    supers = tokens // SUPER
    spans = tokens // SPAN
    row_i = lax.broadcasted_iota(jnp.int32, (SUPER, SUPER), 0)
    col_i = lax.broadcasted_iota(jnp.int32, (SUPER, SUPER), 1)
    same = (row_i >> 6) == (col_i >> 6)
    lower = same & (row_i >= col_i)
    strict = same & (row_i > col_i)
    eye = (row_i == col_i).astype(F32)

    @pl.when(step == 0)
    def _():
        upto = (same & (row_i <= col_i)).astype(F32)
        both = jnp.concatenate([upto, strict.astype(F32)], axis=1)
        pieces = [
            jnp.dot(log_ref[:, s * SUPER:(s + 1) * SUPER], both,
                    precision=lax.Precision.HIGHEST, preferred_element_type=F32)
            for s in range(supers)
        ]
        cum = jnp.concatenate([p[:, :SUPER] for p in pieces], axis=1)
        tail = jnp.concatenate([p[:, SUPER:] for p in pieces], axis=1)
        span_i = lax.broadcasted_iota(jnp.int32, (heads, tokens), 1) >> 6
        keep = jnp.ones((heads, tokens), F32)
        for j in range(spans):
            keep = jnp.where(span_i == j, (1 - flags[j]).astype(F32), keep)
        rows_ref[0] = cum
        rows_ref[1] = jnp.exp(tail)
        rows_ref[2] = jnp.exp(cum) * keep

    units = [(g, s) for g in range(TOGETHER) for s in range(supers)]
    cols, cum_rows, tail_rows, beta_rows = [], [], [], []
    for g in range(TOGETHER):
        head = TOGETHER * (base + stride * step) + g
        take = pl.ds(head, 1)
        beta_row = beta_ref[take, :]
        wanted = [rows_ref[0, take, :], rows_ref[2, take, :], beta_row]
        wanted += [weight_ref[level, take, :] for level in range(9)]
        wanted += [jnp.zeros((4, tokens), F32)]
        c = jnp.transpose(jnp.concatenate(wanted, axis=0))
        cols_ref[g * tokens:(g + 1) * tokens, :] = c
        cols.append(c)
        cum_rows.append(rows_ref[0, take, :])
        tail_rows.append(rows_ref[1, take, :])
        beta_rows.append(beta_row)

    def cut(s):
        return slice(s * SUPER, (s + 1) * SUPER)

    def lanes(g):
        return slice(g * HEAD_DIM, (g + 1) * HEAD_DIM)

    def col(g, s, i):
        return cols[g][cut(s), i:i + 1]

    scores, powers, inverses, right, tails, queries = [], [], [], [], [], []
    for g, s in units:
        q = q_ref[cut(s), lanes(g)]
        k = k_ref[cut(s), lanes(g)]
        k_t = jnp.transpose(k)
        grams = mm(jnp.concatenate([q, k], axis=0), k_t)
        qf, kf, ktf = q.astype(F32), k.astype(F32), k_t.astype(F32)
        rq = lax.rsqrt(jnp.sum(qf * qf, axis=1, keepdims=True) + EPS)
        rk = lax.rsqrt(jnp.sum(kf * kf, axis=1, keepdims=True) + EPS)
        rk_row = lax.rsqrt(jnp.sum(ktf * ktf, axis=0, keepdims=True) + EPS)
        spread = col(g, s, 0) - cum_rows[g][:, cut(s)]
        ratio = jnp.exp(jnp.where(lower, spread, -1e30)) * rk_row
        scores.append((ratio * (rq * grams[:SUPER])).astype(BF16))
        power = jnp.where(strict, (-col(g, s, 2) * rk) * ratio * grams[SUPER:], 0.0)
        inverses.append(eye + power)
        powers.append(power.astype(BF16))
        decay = col(g, s, 1)
        right.append(jnp.concatenate([v_ref[cut(s), lanes(g)], (decay * rk * kf).astype(BF16)], axis=1))
        tails.append((ktf * (rk_row * tail_rows[g][:, cut(s)])).astype(BF16))
        queries.append(decay * rq * qf)

    n = len(units)
    powers = [mm(p, p).astype(BF16) for p in powers]
    for _ in range(4):
        both = [mm(powers[u], jnp.concatenate([powers[u], inverses[u].astype(BF16)], axis=1)) for u in range(n)]
        powers = [b[:, :SUPER].astype(BF16) for b in both]
        inverses = [inverses[u] + both[u][:, SUPER:] for u in range(n)]
    inverses = [inverses[u] + mm(powers[u], inverses[u].astype(BF16)) for u in range(n)]
    solved = []
    for u, (g, s) in enumerate(units):
        scaled = (inverses[u] * beta_rows[g][:, cut(s)]).astype(BF16)
        solved.append(mm(scaled, right[u]).astype(BF16))
    leaves = [[] for _ in range(TOGETHER)]
    for u, (g, s) in enumerate(units):
        for half in range(SUPER // SPAN):
            a, b = half * SPAN, (half + 1) * SPAN
            summary = mm(tails[u][:, a:b], solved[u][a:b, :])
            t = s * SUPER + b - 1
            last = jnp.broadcast_to(cols[g][t:t + 1, 1:2], (1, HEAD_DIM))
            leaves[g].append((summary[:, :HEAD_DIM], summary[:, HEAD_DIM:], last))
    outs = [[] for _ in range(TOGETHER)]
    readers = [[] for _ in range(TOGETHER)]
    for u, (g, s) in enumerate(units):
        read = mm(scores[u], solved[u])
        out = col(g, s, 3) * read[:, :HEAD_DIM]
        reader = queries[u] - read[:, HEAD_DIM:]
        for half in range(SUPER // SPAN):
            a, b = half * SPAN, (half + 1) * SPAN
            outs[g].append(out[a:b])
            readers[g].append(reader[a:b])

    for level in range(1, LOCAL_LEVELS):
        for g in range(TOGETHER):
            maps = leaves[g]
            new_outs, new_readers, new_maps = [], [], []
            for i in range(0, len(maps), 2):
                (s_lo, e_lo, d_lo), (s_hi, e_hi, d_hi) = maps[i], maps[i + 1]
                r_hi = readers[g][i + 1]
                m = r_hi.shape[0]
                t0 = (i + 1) * m
                w_c = cols[g][t0:t0 + m, 3 + level:4 + level]
                both = mm(jnp.concatenate([r_hi.astype(BF16), e_hi.astype(BF16)], axis=0),
                          jnp.concatenate([s_lo.astype(BF16), e_lo.astype(BF16)], axis=1))
                new_outs.append(jnp.concatenate(
                    [outs[g][i], outs[g][i + 1] + w_c * both[:m, :HEAD_DIM]], axis=0))
                new_readers.append(jnp.concatenate(
                    [readers[g][i], d_lo * r_hi - both[:m, HEAD_DIM:]], axis=0))
                new_maps.append((d_hi * s_lo + s_hi - both[m:, :HEAD_DIM],
                                 d_hi * e_lo + d_lo * e_hi - both[m:, HEAD_DIM:],
                                 d_lo * d_hi))
            outs[g], readers[g], leaves[g] = new_outs, new_readers, new_maps
    for g in range(TOGETHER):
        total, erase, decay = leaves[g][0]
        near_ref[:, lanes(g)] = outs[g][0]
        far_ref[:, lanes(g)] = readers[g][0].astype(BF16)
        map_ref[g] = jnp.concatenate([total, eye * decay - erase], axis=1).astype(BF16)


def local_part(base, stride, steps, flags, queries, keys, values, log_decay, beta, weights):
    tokens = queries.shape[0]
    heads = log_decay.shape[0]
    wide = TOGETHER * HEAD_DIM
    block = pl.BlockSpec((tokens, wide), lambda h, f: (0, base + stride * h))
    out = pl.BlockSpec((tokens, wide), lambda h, f: (0, h))
    whole2 = pl.BlockSpec((heads, tokens), lambda h, f: (0, 0))
    whole3 = pl.BlockSpec(weights.shape, lambda h, f: (0, 0, 0))
    part = steps * TOGETHER
    return pl.pallas_call(
        functools.partial(local_kernel, base, stride),
        grid_spec=pltpu.PrefetchScalarGridSpec(
            num_scalar_prefetch=1,
            grid=(steps,),
            in_specs=[block, block, block, whole2, whole2, whole3],
            out_specs=[out, out,
                       pl.BlockSpec((TOGETHER, HEAD_DIM, 2 * HEAD_DIM), lambda h, f: (h, 0, 0)),
                       pl.BlockSpec((TOGETHER * tokens, 16), lambda h, f: (h, 0))],
            scratch_shapes=[pltpu.VMEM((3, heads, tokens), F32)],
        ),
        out_shape=[
            jax.ShapeDtypeStruct((tokens, part * HEAD_DIM), F32),
            jax.ShapeDtypeStruct((tokens, part * HEAD_DIM), BF16),
            jax.ShapeDtypeStruct((part, HEAD_DIM, 2 * HEAD_DIM), BF16),
            jax.ShapeDtypeStruct((part * tokens, 16), F32),
        ],
        compiler_params=pltpu.CompilerParams(vmem_limit_bytes=14 << 20),
        cost_estimate=pl.CostEstimate(flops=part * 1500000000, bytes_accessed=8 << 20, transcendentals=0),
    )(flags, queries, keys, values, log_decay, beta, weights)


def pair_kernel(bits, *refs):
    core = bits[0]
    cur_ref = refs[-1]
    half = cur_ref.shape[0]
    parts = (len(refs) - 1) // 2
    mine, sib = refs[:parts], refs[parts:2 * parts]

    def run(first, second, offset):
        for g in range(half):
            later = second[offset + g]
            both = mm(later[:, HEAD_DIM:], first[offset + g])
            cur_ref[g, :, :HEAD_DIM] = (both[:, :HEAD_DIM] + later[:, :HEAD_DIM].astype(F32)).astype(BF16)
            cur_ref[g, :, HEAD_DIM:] = both[:, HEAD_DIM:].astype(BF16)

    @pl.when(core == 1)
    def _():
        run(sib[-1], mine[-1], half if parts == 1 else 0)

    @pl.when(core == 0)
    def _():
        run(mine[0], sib[0], 0)


def level_kernel(level, bits, *refs):
    if level == 1:
        sib_ref, cur_ref, new_ref, x_ref, carry_ref = refs
    else:
        sib_ref, cur_ref, carried_ref, new_ref, x_ref, carry_ref = refs
    bit = bits[level]
    half = cur_ref.shape[0]

    def store(g, both, later):
        new_ref[g, :, :HEAD_DIM] = (both[:, :HEAD_DIM] + later[:, :HEAD_DIM].astype(F32)).astype(BF16)
        new_ref[g, :, HEAD_DIM:] = both[:, HEAD_DIM:].astype(BF16)

    @pl.when(bit == 1)
    def _():
        for g in range(half):
            later, sib = cur_ref[g], sib_ref[g]
            if level == 1:
                store(g, mm(later[:, HEAD_DIM:], sib), later)
                x_ref[g] = sib[:, :HEAD_DIM]
                carry_ref[g] = sib[:, HEAD_DIM:]
            else:
                both = mm(jnp.concatenate([later[:, HEAD_DIM:], carried_ref[g]], axis=0), sib)
                store(g, both[:HEAD_DIM], later)
                x_ref[g] = both[HEAD_DIM:, :HEAD_DIM].astype(BF16)
                carry_ref[g] = both[HEAD_DIM:, HEAD_DIM:].astype(BF16)

    @pl.when(bit == 0)
    def _():
        row_i = lax.broadcasted_iota(jnp.int32, (HEAD_DIM, HEAD_DIM), 0)
        col_i = lax.broadcasted_iota(jnp.int32, (HEAD_DIM, HEAD_DIM), 1)
        eye = (row_i == col_i).astype(F32).astype(BF16)
        for g in range(half):
            later = sib_ref[g]
            store(g, mm(later[:, HEAD_DIM:], cur_ref[g]), later)
            x_ref[g] = jnp.zeros((HEAD_DIM, HEAD_DIM), BF16)
            carry_ref[g] = eye if level == 1 else carried_ref[g]


def top_kernel(level, bits, sib_ref, carried_ref, x_ref):
    bit = bits[level]

    @pl.when(bit == 1)
    def _():
        for g in range(x_ref.shape[0]):
            x_ref[g] = mm(carried_ref[g], sib_ref[g]).astype(BF16)

    @pl.when(bit == 0)
    def _():
        x_ref[...] = jnp.zeros(x_ref.shape, BF16)


def small_call(kernel, bits, args, outs):
    return pl.pallas_call(
        kernel,
        grid_spec=pltpu.PrefetchScalarGridSpec(
            num_scalar_prefetch=1,
            grid=(1,),
            in_specs=[pl.BlockSpec(a.shape, lambda i, b, n=a.ndim: (0,) * n) for a in args],
            out_specs=[pl.BlockSpec(o.shape, lambda i, b, n=len(o.shape): (0,) * n) for o in outs],
        ),
        out_shape=outs,
        compiler_params=pltpu.CompilerParams(vmem_limit_bytes=3 << 20),
        cost_estimate=pl.CostEstimate(flops=600000000, bytes_accessed=1 << 20, transcendentals=0),
    )(bits, *args)


def read_kernel(side, fold, slots, norm, bits, near_ref, far_ref, cols_ref, *refs):
    core = bits[0]
    refs = list(refs)
    tokens = near_ref.shape[0]
    first = 3 + LOCAL_LEVELS
    upper = core == 1
    units = [(g, t) for g in range(TOGETHER) for t in range(0, tokens, SUPER)]
    count = range(len(units))

    def lanes(g):
        return slice(g * HEAD_DIM, (g + 1) * HEAD_DIM)

    def cols(g, t, i):
        return cols_ref[g * tokens + t:g * tokens + t + SUPER, i:i + 1]

    fars = [far_ref[t:t + SUPER, lanes(g)] for g, t in units]
    ys = [near_ref[t:t + SUPER, lanes(g)] for g, t in units]
    if fold:
        sib_ref = refs.pop(0)
        both = [mm(fars[u], sib_ref[g]) for u, (g, t) in enumerate(units)]
        ys = [ys[u] + jnp.where(upper, cols(g, t, first) * both[u][:, :HEAD_DIM], 0.0)
              for u, (g, t) in enumerate(units)]
        fars = [jnp.where(upper, both[u][:, HEAD_DIM:].astype(BF16), fars[u]) for u in count]
    if slots:
        mine, other = refs[:len(slots)], refs[len(slots):2 * len(slots)]
        refs = refs[2 * len(slots):]
        is_mine = core == side
        states = [jnp.concatenate([jnp.where(is_mine, m[g], o[g]) for m, o in zip(mine, other)], axis=1)
                  for g in range(TOGETHER)]
        reads = [mm(fars[u], states[g]) for u, (g, t) in enumerate(units)]
        for i, slot in enumerate(slots):
            ys = [ys[u] + cols(g, t, first + slot) * reads[u][:, i * HEAD_DIM:(i + 1) * HEAD_DIM]
                  for u, (g, t) in enumerate(units)]
    if norm:
        gain_ref, z_ref = refs[0], refs[-1]
        for u, (g, t) in enumerate(units):
            scale = lax.rsqrt(jnp.mean(ys[u] * ys[u], axis=1, keepdims=True) + EPS)
            z_ref[t:t + SUPER, lanes(g)] = (ys[u] * scale * gain_ref[:, lanes(g)]).astype(BF16)
        return
    for u, (g, t) in enumerate(units):
        refs[0][t:t + SUPER, lanes(g)] = ys[u]
        if fold:
            refs[1][t:t + SUPER, lanes(g)] = fars[u]


def read_part(bits, side, pair, near, far, cols, sib=None, slots=(), mine=(), other=(), gain=None, before=None):
    tokens = near[0].shape[0]
    wide = TOGETHER * HEAD_DIM
    state = pl.BlockSpec((TOGETHER, HEAD_DIM, HEAD_DIM), lambda h, b: (0, 0, 0))

    def column(index):
        return pl.BlockSpec((tokens, wide), lambda h, b: (0, index))

    in_specs = [column(near[1]), column(far[1]),
                pl.BlockSpec((TOGETHER * tokens, 16), lambda h, b, i=cols[1]: (i, 0))]
    args = [bits, near[0], far[0], cols[0]]
    if sib is not None:
        in_specs.append(pl.BlockSpec((TOGETHER, HEAD_DIM, 2 * HEAD_DIM), lambda h, b, i=sib[1]: (i, 0, 0)))
        args.append(sib[0])
    in_specs += [state] * (2 * len(slots))
    args += [*mine, *other]
    aliases = {}
    if gain is not None:
        in_specs.append(pl.BlockSpec((1, wide), lambda h, b: (0, pair)))
        args.append(gain)
        if before is not None:
            aliases = {len(args): 0}
            args.append(before)
            in_specs.append(pl.BlockSpec(memory_space=pl.ANY))
        out_specs = column(pair)
        out_shape = jax.ShapeDtypeStruct((tokens, gain.shape[1]), BF16)
    else:
        out_specs = [column(0)] + ([column(0)] if sib is not None else [])
        out_shape = [jax.ShapeDtypeStruct((tokens, wide), F32)]
        out_shape += [jax.ShapeDtypeStruct((tokens, wide), BF16)] if sib is not None else []
    return pl.pallas_call(
        functools.partial(read_kernel, side, sib is not None, slots, gain is not None),
        grid_spec=pltpu.PrefetchScalarGridSpec(
            num_scalar_prefetch=1, grid=(1,), in_specs=in_specs, out_specs=out_specs),
        out_shape=out_shape,
        input_output_aliases=aliases,
        compiler_params=pltpu.CompilerParams(vmem_limit_bytes=8 << 20),
        cost_estimate=pl.CostEstimate(flops=1200000000, bytes_accessed=2 << 20, transcendentals=0),
    )(*args)


def partner(value, bit):
    size = lax.axis_size("seq")
    return lax.ppermute(value, "seq", [(i, i ^ (1 << bit)) for i in range(size)])


def order_pieces():
    return [p for i in range(PIECES) for p in (i, PIECES + i)]


def project(z, out_weight):
    size = lax.axis_size("head")
    me = lax.axis_index("head")
    rows = z.shape[0] // size
    cols = out_weight.shape[1] // (2 * PIECES)
    up = [(j, (j + 1) % size) for j in range(size)]
    down = [(j, (j - 1) % size) for j in range(size)]

    def term(block, piece):
        part = lax.dynamic_slice_in_dim(z, (block % size) * rows, rows, 0)
        w = out_weight[:, piece * cols:(piece + 1) * cols]
        return jnp.dot(part, w, preferred_element_type=F32).astype(BF16)

    order = order_pieces()
    sums = {}
    for p in order:
        sums[p] = term(me + size - 1 if p < PIECES else me + 1, p)
    last = None
    for s in range(size - 1):
        got, own = {}, {}
        for p in order:
            got[p] = lax.ppermute(sums[p], "head", up if p < PIECES else down)
            own[p] = term(me + 2 * size - 2 - s if p < PIECES else me + 2 + s, p)
        for p in order:
            keep = (own[p],) if last is None else (own[p], last)
            mine = lax.optimization_barrier(keep)[0]
            last = (got[p].astype(F32) + mine.astype(F32)).astype(BF16)
            sums[p] = last
    return jnp.concatenate([sums[p] for p in range(2 * PIECES)], axis=1)


def body(queries, keys, values, log_decay, beta, level_weights, doc_start, norm_gain, out_weight):
    heads = log_decay.shape[0]
    mine_heads = heads // (2 * CHUNKS)
    nbits = lax.axis_size("seq").bit_length() - 1
    index = lax.axis_index("seq")
    bits = jnp.stack([(index >> b) & 1 for b in range(nbits)]).astype(jnp.int32)
    gain = norm_gain.reshape(1, -1)
    wide = jax.ShapeDtypeStruct((mine_heads, HEAD_DIM, 2 * HEAD_DIM), BF16)
    square = jax.ShapeDtypeStruct((mine_heads, HEAD_DIM, HEAD_DIM), BF16)
    in_hbm = lambda x: pltpu.with_memory_space_constraint(x, pltpu.HBM)
    given = [in_hbm(x) for x in (queries, keys, values, log_decay, beta, level_weights)]
    doc_start = in_hbm(doc_start)

    def local(base, stride, steps, flags):
        near, far, maps, cols = local_part(base, stride, steps, flags, *given)
        return in_hbm(near), in_hbm(far), maps, in_hbm(cols), partner(maps, 0)

    front = local(0, CHUNKS, 2, doc_start)
    low = local(1, CHUNKS, 1, doc_start)
    cur = small_call(pair_kernel, bits, [front[2], front[4]], [wide])[0]
    flags = lax.optimization_barrier((doc_start, cur))[0]
    high = local(3, CHUNKS, 1, flags)
    settled = lax.optimization_barrier((bits, high[2]))[0]
    curs = [cur, small_call(pair_kernel, bits, [low[2], high[2], low[4], high[4]], [wide])[0]]
    where = [[(front, 0), (front, 1)], [(low, 0), (high, 0)]]
    parts = [(c, h) for c in range(CHUNKS) for h in range(2)]
    nears, fars, colss = {}, {}, {}
    for c, h in parts:
        (near, far, _, cols, sib), i = where[c][h]
        colss[c, h] = (cols, i)
        near, far = read_part(settled, h, 2 * h + c, (near, i), (far, i), (cols, i), sib=(sib, i))
        nears[c, h], fars[c, h] = (near, 0), (far, 0)
    carried = [None] * CHUNKS
    states = [[] for _ in range(CHUNKS)]
    others = [[] for _ in range(CHUNKS)]
    for level in range(1, nbits):
        for c in range(CHUNKS):
            if level < nbits - 1:
                sib = partner(curs[c], level)
                args = [sib, curs[c]] if level == 1 else [sib, curs[c], carried[c]]
                curs[c], x, carried[c] = small_call(
                    functools.partial(level_kernel, level), bits, args, [wide, square, square])
            else:
                sib = partner(curs[c][:, :, :HEAD_DIM], level)
                x = small_call(functools.partial(top_kernel, level), bits, [sib, carried[c]], [square])[0]
            states[c].append(x)
            others[c].append(partner(x, 0))
    z = None
    early = (nbits - 1) // 2
    for c, h in parts:
        near = read_part(bits, h, 2 * h + c, nears[c, h], fars[c, h], colss[c, h],
                         slots=tuple(range(1, early + 1)), mine=states[c][:early], other=others[c][:early])[0]
        nears[c, h] = (near, 0)
    for c, h in parts:
        z = read_part(bits, h, 2 * h + c, nears[c, h], fars[c, h], colss[c, h],
                      slots=tuple(range(early + 1, nbits)), mine=states[c][early:], other=others[c][early:],
                      gain=gain, before=z)
    return project(z, out_weight)


def solution(mesh):
    placed = (
        P("seq", "head"),
        P("seq", "head"),
        P("seq", "head"),
        P("head", "seq"),
        P("head", "seq"),
        P(None, "head", "seq"),
        P("seq"),
        P("head"),
        P("head", None),
    )
    return jax.shard_map(
        body, mesh=mesh, in_specs=placed, out_specs=P(("seq", "head"), None), check_vma=False
    )
```

```python
import functools
import jax
import jax.numpy as jnp
from jax import lax
from jax.experimental import pallas as pl
from jax.experimental.pallas import tpu as pltpu
from jax.sharding import PartitionSpec as P


SPAN = 64
SUPER = 128
HEAD_DIM = 128
LOCAL_LEVELS = 4
TOGETHER = 2
CHUNKS = 2
PIECES = 2
EPS = 1e-06
F32 = jnp.float32
BF16 = jnp.bfloat16


def mm(a, b):
    return jnp.dot(a, b, preferred_element_type=F32)


def local_kernel(base, stride, flags, q_ref, k_ref, v_ref, log_ref, beta_ref, weight_ref,
                 near_ref, far_ref, map_ref, rows_ref):
    step = pl.program_id(0)
    tokens = q_ref.shape[0]
    heads = log_ref.shape[0]
    supers = tokens // SUPER
    spans = tokens // SPAN
    row_i = lax.broadcasted_iota(jnp.int32, (SUPER, SUPER), 0)
    col_i = lax.broadcasted_iota(jnp.int32, (SUPER, SUPER), 1)
    same = (row_i >> 6) == (col_i >> 6)
    lower = same & (row_i >= col_i)
    strict = same & (row_i > col_i)
    eye = (row_i == col_i).astype(F32)

    @pl.when(step == 0)
    def _():
        upto = (same & (row_i <= col_i)).astype(F32)
        both = jnp.concatenate([upto, strict.astype(F32)], axis=1)
        pieces = [
            jnp.dot(log_ref[:, s * SUPER:(s + 1) * SUPER], both,
                    precision=lax.Precision.HIGHEST, preferred_element_type=F32)
            for s in range(supers)
        ]
        cum = jnp.concatenate([p[:, :SUPER] for p in pieces], axis=1)
        tail = jnp.concatenate([p[:, SUPER:] for p in pieces], axis=1)
        span_i = lax.broadcasted_iota(jnp.int32, (heads, tokens), 1) >> 6
        keep = jnp.ones((heads, tokens), F32)
        for j in range(spans):
            keep = jnp.where(span_i == j, (1 - flags[j]).astype(F32), keep)
        rows_ref[0] = cum
        rows_ref[1] = jnp.exp(tail)
        rows_ref[2] = jnp.exp(cum) * keep

    units = [(g, s) for g in range(TOGETHER) for s in range(supers)]
    cols, cum_rows, tail_rows, beta_rows = [], [], [], []
    for g in range(TOGETHER):
        head = TOGETHER * (base + stride * step) + g
        take = pl.ds(head, 1)
        beta_row = beta_ref[take, :]
        wanted = [rows_ref[0, take, :], rows_ref[2, take, :], beta_row]
        wanted += [weight_ref[level, take, :] for level in range(LOCAL_LEVELS)]
        wanted += [jnp.zeros((1, tokens), F32)]
        c = jnp.transpose(jnp.concatenate(wanted, axis=0))
        cols.append(c)
        cum_rows.append(rows_ref[0, take, :])
        tail_rows.append(rows_ref[1, take, :])
        beta_rows.append(beta_row)

    def cut(s):
        return slice(s * SUPER, (s + 1) * SUPER)

    def lanes(g):
        return slice(g * HEAD_DIM, (g + 1) * HEAD_DIM)

    def col(g, s, i):
        return cols[g][cut(s), i:i + 1]

    scores, powers, inverses, right, tails, queries = [], [], [], [], [], []
    for g, s in units:
        q = q_ref[cut(s), lanes(g)]
        k = k_ref[cut(s), lanes(g)]
        k_t = jnp.transpose(k)
        grams = mm(jnp.concatenate([q, k], axis=0), k_t)
        qf, kf, ktf = q.astype(F32), k.astype(F32), k_t.astype(F32)
        rq = lax.rsqrt(jnp.sum(qf * qf, axis=1, keepdims=True) + EPS)
        rk = lax.rsqrt(jnp.sum(kf * kf, axis=1, keepdims=True) + EPS)
        rk_row = lax.rsqrt(jnp.sum(ktf * ktf, axis=0, keepdims=True) + EPS)
        spread = col(g, s, 0) - cum_rows[g][:, cut(s)]
        ratio = jnp.exp(jnp.where(lower, spread, -1e30)) * rk_row
        scores.append((ratio * (rq * grams[:SUPER])).astype(BF16))
        power = jnp.where(strict, (-col(g, s, 2) * rk) * ratio * grams[SUPER:], 0.0)
        inverses.append(eye + power)
        powers.append(power.astype(BF16))
        decay = col(g, s, 1)
        right.append(jnp.concatenate([v_ref[cut(s), lanes(g)], (decay * rk * kf).astype(BF16)], axis=1))
        tails.append((ktf * (rk_row * tail_rows[g][:, cut(s)])).astype(BF16))
        queries.append(decay * rq * qf)

    n = len(units)
    powers = [mm(p, p).astype(BF16) for p in powers]
    for _ in range(4):
        both = [mm(powers[u], jnp.concatenate([powers[u], inverses[u].astype(BF16)], axis=1)) for u in range(n)]
        powers = [b[:, :SUPER].astype(BF16) for b in both]
        inverses = [inverses[u] + both[u][:, SUPER:] for u in range(n)]
    inverses = [inverses[u] + mm(powers[u], inverses[u].astype(BF16)) for u in range(n)]
    solved = []
    for u, (g, s) in enumerate(units):
        scaled = (inverses[u] * beta_rows[g][:, cut(s)]).astype(BF16)
        solved.append(mm(scaled, right[u]).astype(BF16))
    leaves = [[] for _ in range(TOGETHER)]
    for u, (g, s) in enumerate(units):
        for half in range(SUPER // SPAN):
            a, b = half * SPAN, (half + 1) * SPAN
            summary = mm(tails[u][:, a:b], solved[u][a:b, :])
            t = s * SUPER + b - 1
            last = jnp.broadcast_to(cols[g][t:t + 1, 1:2], (1, HEAD_DIM))
            leaves[g].append((summary[:, :HEAD_DIM], summary[:, HEAD_DIM:], last))
    outs = [[] for _ in range(TOGETHER)]
    readers = [[] for _ in range(TOGETHER)]
    for u, (g, s) in enumerate(units):
        read = mm(scores[u], solved[u])
        out = col(g, s, 3) * read[:, :HEAD_DIM]
        reader = queries[u] - read[:, HEAD_DIM:]
        for half in range(SUPER // SPAN):
            a, b = half * SPAN, (half + 1) * SPAN
            outs[g].append(out[a:b])
            readers[g].append(reader[a:b])

    for level in range(1, LOCAL_LEVELS):
        for g in range(TOGETHER):
            maps = leaves[g]
            new_outs, new_readers, new_maps = [], [], []
            for i in range(0, len(maps), 2):
                (s_lo, e_lo, d_lo), (s_hi, e_hi, d_hi) = maps[i], maps[i + 1]
                r_hi = readers[g][i + 1]
                m = r_hi.shape[0]
                t0 = (i + 1) * m
                w_c = cols[g][t0:t0 + m, 3 + level:4 + level]
                both = mm(jnp.concatenate([r_hi.astype(BF16), e_hi.astype(BF16)], axis=0),
                          jnp.concatenate([s_lo.astype(BF16), e_lo.astype(BF16)], axis=1))
                new_outs.append(jnp.concatenate(
                    [outs[g][i], outs[g][i + 1] + w_c * both[:m, :HEAD_DIM]], axis=0))
                new_readers.append(jnp.concatenate(
                    [readers[g][i], d_lo * r_hi - both[:m, HEAD_DIM:]], axis=0))
                new_maps.append((d_hi * s_lo + s_hi - both[m:, :HEAD_DIM],
                                 d_hi * e_lo + d_lo * e_hi - both[m:, HEAD_DIM:],
                                 d_lo * d_hi))
            outs[g], readers[g], leaves[g] = new_outs, new_readers, new_maps
    for g in range(TOGETHER):
        total, erase, decay = leaves[g][0]
        near_ref[:, lanes(g)] = outs[g][0]
        far_ref[:, lanes(g)] = readers[g][0].astype(BF16)
        map_ref[g] = jnp.concatenate([total, eye * decay - erase], axis=1).astype(BF16)


def local_part(base, stride, steps, flags, queries, keys, values, log_decay, beta, weights):
    tokens = queries.shape[0]
    heads = log_decay.shape[0]
    wide = TOGETHER * HEAD_DIM
    block = pl.BlockSpec((tokens, wide), lambda h, f: (0, base + stride * h))
    out = pl.BlockSpec((tokens, wide), lambda h, f: (0, h))
    whole2 = pl.BlockSpec((heads, tokens), lambda h, f: (0, 0))
    whole3 = pl.BlockSpec(weights.shape, lambda h, f: (0, 0, 0))
    part = steps * TOGETHER
    return pl.pallas_call(
        functools.partial(local_kernel, base, stride),
        grid_spec=pltpu.PrefetchScalarGridSpec(
            num_scalar_prefetch=1,
            grid=(steps,),
            in_specs=[block, block, block, whole2, whole2, whole3],
            out_specs=[out, out,
                       pl.BlockSpec((TOGETHER, HEAD_DIM, 2 * HEAD_DIM), lambda h, f: (h, 0, 0))],
            scratch_shapes=[pltpu.VMEM((3, heads, tokens), F32)],
        ),
        out_shape=[
            pltpu.HBM((tokens, part * HEAD_DIM), F32),
            pltpu.HBM((tokens, part * HEAD_DIM), BF16),
            jax.ShapeDtypeStruct((part, HEAD_DIM, 2 * HEAD_DIM), BF16),
        ],
        compiler_params=pltpu.CompilerParams(vmem_limit_bytes=14 << 20),
        cost_estimate=pl.CostEstimate(flops=part * 1500000000, bytes_accessed=8 << 20, transcendentals=0),
    )(flags, queries, keys, values, log_decay, beta, weights)


def pair_kernel(bits, *refs):
    core = bits[0]
    cur_ref = refs[-1]
    half = cur_ref.shape[0]
    parts = (len(refs) - 1) // 2
    mine, sib = refs[:parts], refs[parts:2 * parts]

    def run(first, second, offset):
        for g in range(half):
            later = second[offset + g]
            both = mm(later[:, HEAD_DIM:], first[offset + g])
            cur_ref[g, :, :HEAD_DIM] = (both[:, :HEAD_DIM] + later[:, :HEAD_DIM].astype(F32)).astype(BF16)
            cur_ref[g, :, HEAD_DIM:] = both[:, HEAD_DIM:].astype(BF16)

    @pl.when(core == 1)
    def _():
        run(sib[-1], mine[-1], half if parts == 1 else 0)

    @pl.when(core == 0)
    def _():
        run(mine[0], sib[0], 0)


def level_kernel(level, bits, *refs):
    if level == 1:
        sib_ref, cur_ref, new_ref, x_ref, carry_ref = refs
    else:
        sib_ref, cur_ref, carried_ref, new_ref, x_ref, carry_ref = refs
    bit = bits[level]
    half = cur_ref.shape[0]

    def store(g, both, later):
        new_ref[g, :, :HEAD_DIM] = (both[:, :HEAD_DIM] + later[:, :HEAD_DIM].astype(F32)).astype(BF16)
        new_ref[g, :, HEAD_DIM:] = both[:, HEAD_DIM:].astype(BF16)

    @pl.when(bit == 1)
    def _():
        for g in range(half):
            later, sib = cur_ref[g], sib_ref[g]
            if level == 1:
                store(g, mm(later[:, HEAD_DIM:], sib), later)
                x_ref[g] = sib[:, :HEAD_DIM]
                carry_ref[g] = sib[:, HEAD_DIM:]
            else:
                both = mm(jnp.concatenate([later[:, HEAD_DIM:], carried_ref[g]], axis=0), sib)
                store(g, both[:HEAD_DIM], later)
                x_ref[g] = both[HEAD_DIM:, :HEAD_DIM].astype(BF16)
                carry_ref[g] = both[HEAD_DIM:, HEAD_DIM:].astype(BF16)

    @pl.when(bit == 0)
    def _():
        row_i = lax.broadcasted_iota(jnp.int32, (HEAD_DIM, HEAD_DIM), 0)
        col_i = lax.broadcasted_iota(jnp.int32, (HEAD_DIM, HEAD_DIM), 1)
        eye = (row_i == col_i).astype(F32).astype(BF16)
        for g in range(half):
            later = sib_ref[g]
            store(g, mm(later[:, HEAD_DIM:], cur_ref[g]), later)
            x_ref[g] = jnp.zeros((HEAD_DIM, HEAD_DIM), BF16)
            carry_ref[g] = eye if level == 1 else carried_ref[g]


def top_kernel(level, bits, sib_ref, carried_ref, x_ref):
    bit = bits[level]

    @pl.when(bit == 1)
    def _():
        for g in range(x_ref.shape[0]):
            x_ref[g] = mm(carried_ref[g], sib_ref[g]).astype(BF16)

    @pl.when(bit == 0)
    def _():
        x_ref[...] = jnp.zeros(x_ref.shape, BF16)


def small_call(kernel, bits, args, outs):
    return pl.pallas_call(
        kernel,
        grid_spec=pltpu.PrefetchScalarGridSpec(
            num_scalar_prefetch=1,
            grid=(1,),
            in_specs=[pl.BlockSpec(a.shape, lambda i, b, n=a.ndim: (0,) * n) for a in args],
            out_specs=[pl.BlockSpec(o.shape, lambda i, b, n=len(o.shape): (0,) * n) for o in outs],
        ),
        out_shape=outs,
        compiler_params=pltpu.CompilerParams(vmem_limit_bytes=3 << 20),
        cost_estimate=pl.CostEstimate(flops=600000000, bytes_accessed=1 << 20, transcendentals=0),
    )(bits, *args)


def final_kernel(levels, parts, chunk, bits, *refs):
    core = bits[0]
    refs = list(refs)
    near_refs = [refs.pop(0) for _ in range(parts)]
    far_refs = [refs.pop(0) for _ in range(parts)]
    sib_refs = [refs.pop(0) for _ in range(parts)]
    weight_ref, gain_ref = refs[:2]
    mine, other, z_ref = refs[2:2 + levels], refs[2 + levels:2 + 2 * levels], refs[-1]
    tokens = near_refs[0].shape[0]
    side = pl.program_id(0)
    is_mine = side == core
    upper = core == 1
    first = LOCAL_LEVELS

    def lanes(g):
        return slice(g * HEAD_DIM, (g + 1) * HEAD_DIM)

    def pick(group, where):
        if parts == 1:
            return group[0][where]
        return jnp.where(side == 0, group[0][where], group[1][where])

    stacks = []
    for g in range(TOGETHER):
        sib = pick(sib_refs, g)
        states = jnp.concatenate([jnp.where(is_mine, m[g], o[g]) for m, o in zip(mine, other)], axis=1)
        states = jnp.where(upper, mm(sib[:, HEAD_DIM:], states).astype(BF16), states)
        low = jnp.where(upper, sib[:, :HEAD_DIM], jnp.zeros((HEAD_DIM, HEAD_DIM), BF16))
        stacks.append(jnp.transpose(jnp.concatenate([low, states], axis=1)))
    step = 2 * SUPER
    units = [(g, t) for g in range(TOGETHER) for t in range(0, tokens, step)]
    reads = [lax.dot_general(stacks[g], pick(far_refs, (slice(t, t + step), lanes(g))),
                             (((1,), (1,)), ((), ())), preferred_element_type=F32) for g, t in units]
    for u, (g, t) in enumerate(units):
        head = TOGETHER * (CHUNKS * side + chunk) + g
        turned = None
        for i in range(levels + 1):
            term = weight_ref[first + i, pl.ds(head, 1), t:t + step] * reads[u][i * HEAD_DIM:(i + 1) * HEAD_DIM]
            turned = term if turned is None else turned + term
        y = pick(near_refs, (slice(t, t + step), lanes(g))) + jnp.transpose(turned)
        scale = lax.rsqrt(jnp.mean(y * y, axis=1, keepdims=True) + EPS)
        z_ref[t:t + step, lanes(g)] = (y * scale * gain_ref[:, lanes(g)]).astype(BF16)


def final_part(chunk, bits, nears, fars, sibs, weights, gain, mine, other, before):
    tokens = nears[0].shape[0]
    wide = TOGETHER * HEAD_DIM
    levels = len(mine)
    parts = len(nears)
    placed = lambda h, b: (0, CHUNKS * h + chunk)
    state = pl.BlockSpec((TOGETHER, HEAD_DIM, HEAD_DIM), lambda h, b: (0, 0, 0))
    if parts == 1:
        block = pl.BlockSpec((tokens, wide), lambda h, b: (0, h))
        maps = pl.BlockSpec((TOGETHER, HEAD_DIM, 2 * HEAD_DIM), lambda h, b: (h, 0, 0))
    else:
        block = pl.BlockSpec((tokens, wide), lambda h, b: (0, 0))
        maps = pl.BlockSpec((TOGETHER, HEAD_DIM, 2 * HEAD_DIM), lambda h, b: (0, 0, 0))
    in_specs = [block] * (2 * parts) + [maps] * parts
    in_specs += [pl.BlockSpec(weights.shape, lambda h, b: (0, 0, 0)), pl.BlockSpec((1, wide), placed)]
    in_specs += [state] * (2 * levels)
    args = [bits, *nears, *fars, *sibs, weights, gain, *mine, *other]
    aliases = {}
    if before is not None:
        aliases = {len(args): 0}
        args.append(before)
        in_specs.append(pl.BlockSpec(memory_space=pl.ANY))
    return pl.pallas_call(
        functools.partial(final_kernel, levels, parts, chunk),
        grid_spec=pltpu.PrefetchScalarGridSpec(
            num_scalar_prefetch=1,
            grid=(2,),
            in_specs=in_specs,
            out_specs=pl.BlockSpec((tokens, wide), placed),
        ),
        out_shape=jax.ShapeDtypeStruct((tokens, gain.shape[1]), BF16),
        input_output_aliases=aliases,
        compiler_params=pltpu.CompilerParams(vmem_limit_bytes=14 << 20),
        cost_estimate=pl.CostEstimate(flops=2400000000, bytes_accessed=4 << 20, transcendentals=0),
    )(*args)


def partner(value, bit):
    size = lax.axis_size("seq")
    return lax.ppermute(value, "seq", [(i, i ^ (1 << bit)) for i in range(size)])


def order_pieces():
    return [p for i in range(PIECES) for p in (i, PIECES + i)]


def project(z, out_weight):
    size = lax.axis_size("head")
    me = lax.axis_index("head")
    rows = z.shape[0] // size
    cols = out_weight.shape[1] // (2 * PIECES)
    up = [(j, (j + 1) % size) for j in range(size)]
    down = [(j, (j - 1) % size) for j in range(size)]

    def term(block, piece):
        part = lax.dynamic_slice_in_dim(z, (block % size) * rows, rows, 0)
        w = out_weight[:, piece * cols:(piece + 1) * cols]
        return jnp.dot(part, w, preferred_element_type=F32).astype(BF16)

    order = order_pieces()
    sums = {}
    for p in order:
        sums[p] = term(me + size - 1 if p < PIECES else me + 1, p)
    last = None
    for s in range(size - 1):
        got, own = {}, {}
        for p in order:
            got[p] = lax.ppermute(sums[p], "head", up if p < PIECES else down)
            own[p] = term(me + 2 * size - 2 - s if p < PIECES else me + 2 + s, p)
        for p in order:
            keep = (own[p],) if last is None else (own[p], last)
            mine = lax.optimization_barrier(keep)[0]
            last = (got[p].astype(F32) + mine.astype(F32)).astype(BF16)
            sums[p] = last
    return jnp.concatenate([sums[p] for p in range(2 * PIECES)], axis=1)


def layer(queries, keys, values, log_decay, beta, level_weights, doc_start, norm_gain, out_weight):
    heads = log_decay.shape[0]
    mine_heads = heads // (2 * CHUNKS)
    nbits = lax.axis_size("seq").bit_length() - 1
    index = lax.axis_index("seq")
    bits = jnp.stack([(index >> b) & 1 for b in range(nbits)]).astype(jnp.int32)
    gain = norm_gain.reshape(1, -1)
    wide = jax.ShapeDtypeStruct((mine_heads, HEAD_DIM, 2 * HEAD_DIM), BF16)
    square = jax.ShapeDtypeStruct((mine_heads, HEAD_DIM, HEAD_DIM), BF16)
    in_hbm = lambda x: pltpu.with_memory_space_constraint(x, pltpu.HBM)
    given = [in_hbm(x) for x in (queries, keys, values, log_decay, beta, level_weights)]
    doc_start = in_hbm(doc_start)

    def local(base, stride, steps, flags):
        near, far, maps = local_part(base, stride, steps, flags, *given)
        return near, far, maps, partner(maps, 0)

    front = local(0, CHUNKS, 2, doc_start)
    low = local(1, CHUNKS, 1, doc_start)
    cur = small_call(pair_kernel, bits, [front[2], front[3]], [wide])[0]
    flags = lax.optimization_barrier((doc_start, cur))[0]
    high = local(3, CHUNKS, 1, flags)
    curs = [cur, small_call(pair_kernel, bits, [low[2], high[2], low[3], high[3]], [wide])[0]]
    sources = [[front], [low, high]]
    carried = [None] * CHUNKS
    states = [[] for _ in range(CHUNKS)]
    others = [[] for _ in range(CHUNKS)]
    for level in range(1, nbits):
        for c in range(CHUNKS):
            if level < nbits - 1:
                sib = partner(curs[c], level)
                args = [sib, curs[c]] if level == 1 else [sib, curs[c], carried[c]]
                curs[c], x, carried[c] = small_call(
                    functools.partial(level_kernel, level), bits, args, [wide, square, square])
            else:
                sib = partner(curs[c][:, :, :HEAD_DIM], level)
                x = small_call(functools.partial(top_kernel, level), bits, [sib, carried[c]], [square])[0]
            states[c].append(x)
            others[c].append(partner(x, 0))
    z = None
    for c in range(CHUNKS):
        nears, fars, _, sibs = zip(*sources[c])
        z = final_part(c, bits, nears, fars, sibs, given[5], gain, states[c], others[c], z)
    return project(z, out_weight)


def solution(mesh):
    placed = (
        P("seq", "head"),
        P("seq", "head"),
        P("seq", "head"),
        P("head", "seq"),
        P("head", "seq"),
        P(None, "head", "seq"),
        P("seq"),
        P("head"),
        P("head", None),
    )
    return jax.shard_map(layer, mesh=mesh, in_specs=placed, out_specs=P(("seq", "head"), None), check_vma=False)
```

```python
import functools
import jax
import jax.numpy as jnp
from jax import lax
from jax.experimental import pallas as pl
from jax.experimental.pallas import tpu as pltpu
from jax.sharding import PartitionSpec as P


SPAN = 64
SUPER = 128
HEAD_DIM = 128
LOCAL_LEVELS = 4
TOGETHER = 2
GROUP = 8
CHIPS = 4
PIECES = 2
EPS = 1e-06
F32 = jnp.float32
BF16 = jnp.bfloat16


def mm(a, b):
    return jnp.dot(a, b, preferred_element_type=F32)


def local_kernel(flags, q_ref, k_ref, v_ref, log_ref, beta_ref, weight_ref,
                 near_ref, far_ref, map_ref, rows_ref):
    step = pl.program_id(0)
    tokens = q_ref.shape[0]
    heads = log_ref.shape[0]
    supers = tokens // SUPER
    spans = tokens // SPAN
    row_i = lax.broadcasted_iota(jnp.int32, (SUPER, SUPER), 0)
    col_i = lax.broadcasted_iota(jnp.int32, (SUPER, SUPER), 1)
    same = (row_i >> 6) == (col_i >> 6)
    lower = same & (row_i >= col_i)
    strict = same & (row_i > col_i)
    eye = (row_i == col_i).astype(F32)

    @pl.when(step == 0)
    def _():
        upto = (same & (row_i <= col_i)).astype(F32)
        both = jnp.concatenate([upto, strict.astype(F32)], axis=1)
        pieces = [
            jnp.dot(log_ref[:, s * SUPER:(s + 1) * SUPER], both,
                    precision=lax.Precision.HIGHEST, preferred_element_type=F32)
            for s in range(supers)
        ]
        cum = jnp.concatenate([p[:, :SUPER] for p in pieces], axis=1)
        tail = jnp.concatenate([p[:, SUPER:] for p in pieces], axis=1)
        span_i = lax.broadcasted_iota(jnp.int32, (heads, tokens), 1) >> 6
        keep = jnp.ones((heads, tokens), F32)
        for j in range(spans):
            keep = jnp.where(span_i == j, (1 - flags[j]).astype(F32), keep)
        rows_ref[0] = cum
        rows_ref[1] = jnp.exp(tail)
        rows_ref[2] = jnp.exp(cum) * keep

    units = [(g, s) for g in range(TOGETHER) for s in range(supers)]
    cols, cum_rows, tail_rows, beta_rows = [], [], [], []
    for g in range(TOGETHER):
        head = TOGETHER * step + g
        take = pl.ds(head, 1)
        beta_row = beta_ref[take, :]
        wanted = [rows_ref[0, take, :], rows_ref[2, take, :], beta_row]
        wanted += [weight_ref[level, take, :] for level in range(LOCAL_LEVELS)]
        wanted += [jnp.zeros((1, tokens), F32)]
        c = jnp.transpose(jnp.concatenate(wanted, axis=0))
        cols.append(c)
        cum_rows.append(rows_ref[0, take, :])
        tail_rows.append(rows_ref[1, take, :])
        beta_rows.append(beta_row)

    def cut(s):
        return slice(s * SUPER, (s + 1) * SUPER)

    def lanes(g):
        return slice(g * HEAD_DIM, (g + 1) * HEAD_DIM)

    def col(g, s, i):
        return cols[g][cut(s), i:i + 1]

    scores, powers, inverses, right, tails, queries = [], [], [], [], [], []
    for g, s in units:
        q = q_ref[cut(s), lanes(g)]
        k = k_ref[cut(s), lanes(g)]
        k_t = jnp.transpose(k)
        grams = mm(jnp.concatenate([q, k], axis=0), k_t)
        qf, kf, ktf = q.astype(F32), k.astype(F32), k_t.astype(F32)
        rq = lax.rsqrt(jnp.sum(qf * qf, axis=1, keepdims=True) + EPS)
        rk = lax.rsqrt(jnp.sum(kf * kf, axis=1, keepdims=True) + EPS)
        rk_row = lax.rsqrt(jnp.sum(ktf * ktf, axis=0, keepdims=True) + EPS)
        spread = col(g, s, 0) - cum_rows[g][:, cut(s)]
        ratio = jnp.exp(jnp.where(lower, spread, -1e30)) * rk_row
        scores.append((ratio * (rq * grams[:SUPER])).astype(BF16))
        power = jnp.where(strict, (-col(g, s, 2) * rk) * ratio * grams[SUPER:], 0.0)
        inverses.append(eye + power)
        powers.append(power.astype(BF16))
        decay = col(g, s, 1)
        right.append(jnp.concatenate([v_ref[cut(s), lanes(g)], (decay * rk * kf).astype(BF16)], axis=1))
        tails.append((ktf * (rk_row * tail_rows[g][:, cut(s)])).astype(BF16))
        queries.append(decay * rq * qf)

    n = len(units)
    powers = [mm(p, p).astype(BF16) for p in powers]
    for _ in range(4):
        both = [mm(powers[u], jnp.concatenate([powers[u], inverses[u].astype(BF16)], axis=1)) for u in range(n)]
        powers = [b[:, :SUPER].astype(BF16) for b in both]
        inverses = [inverses[u] + both[u][:, SUPER:] for u in range(n)]
    inverses = [inverses[u] + mm(powers[u], inverses[u].astype(BF16)) for u in range(n)]
    solved = []
    for u, (g, s) in enumerate(units):
        scaled = (inverses[u] * beta_rows[g][:, cut(s)]).astype(BF16)
        solved.append(mm(scaled, right[u]).astype(BF16))
    leaves = [[] for _ in range(TOGETHER)]
    for u, (g, s) in enumerate(units):
        for half in range(SUPER // SPAN):
            a, b = half * SPAN, (half + 1) * SPAN
            summary = mm(tails[u][:, a:b], solved[u][a:b, :])
            t = s * SUPER + b - 1
            last = jnp.broadcast_to(cols[g][t:t + 1, 1:2], (1, HEAD_DIM))
            leaves[g].append((summary[:, :HEAD_DIM], summary[:, HEAD_DIM:], last))
    outs = [[] for _ in range(TOGETHER)]
    readers = [[] for _ in range(TOGETHER)]
    for u, (g, s) in enumerate(units):
        read = mm(scores[u], solved[u])
        out = col(g, s, 3) * read[:, :HEAD_DIM]
        reader = queries[u] - read[:, HEAD_DIM:]
        for half in range(SUPER // SPAN):
            a, b = half * SPAN, (half + 1) * SPAN
            outs[g].append(out[a:b])
            readers[g].append(reader[a:b])

    for level in range(1, LOCAL_LEVELS):
        for g in range(TOGETHER):
            maps = leaves[g]
            new_outs, new_readers, new_maps = [], [], []
            for i in range(0, len(maps), 2):
                (s_lo, e_lo, d_lo), (s_hi, e_hi, d_hi) = maps[i], maps[i + 1]
                r_hi = readers[g][i + 1]
                m = r_hi.shape[0]
                t0 = (i + 1) * m
                w_c = cols[g][t0:t0 + m, 3 + level:4 + level]
                both = mm(jnp.concatenate([r_hi.astype(BF16), e_hi.astype(BF16)], axis=0),
                          jnp.concatenate([s_lo.astype(BF16), e_lo.astype(BF16)], axis=1))
                new_outs.append(jnp.concatenate(
                    [outs[g][i], outs[g][i + 1] + w_c * both[:m, :HEAD_DIM]], axis=0))
                new_readers.append(jnp.concatenate(
                    [readers[g][i], d_lo * r_hi - both[:m, HEAD_DIM:]], axis=0))
                new_maps.append((d_hi * s_lo + s_hi - both[m:, :HEAD_DIM],
                                 d_hi * e_lo + d_lo * e_hi - both[m:, HEAD_DIM:],
                                 d_lo * d_hi))
            outs[g], readers[g], leaves[g] = new_outs, new_readers, new_maps
    for g in range(TOGETHER):
        total, erase, decay = leaves[g][0]
        near_ref[:, lanes(g)] = outs[g][0]
        far_ref[:, lanes(g)] = readers[g][0].astype(BF16)
        map_ref[g] = jnp.concatenate([total, eye * decay - erase], axis=1).astype(BF16)


def local_part(flags, queries, keys, values, log_decay, beta, weights):
    tokens = queries.shape[0]
    heads = log_decay.shape[0]
    wide = TOGETHER * HEAD_DIM
    steps = heads // TOGETHER
    block = pl.BlockSpec((tokens, wide), lambda h, f: (0, h))
    out = block
    whole2 = pl.BlockSpec((heads, tokens), lambda h, f: (0, 0))
    whole3 = pl.BlockSpec(weights.shape, lambda h, f: (0, 0, 0))
    part = steps * TOGETHER
    return pl.pallas_call(
        local_kernel,
        grid_spec=pltpu.PrefetchScalarGridSpec(
            num_scalar_prefetch=1,
            grid=(steps,),
            in_specs=[block, block, block, whole2, whole2, whole3],
            out_specs=[out, out,
                       pl.BlockSpec((TOGETHER, HEAD_DIM, 2 * HEAD_DIM), lambda h, f: (h, 0, 0))],
            scratch_shapes=[pltpu.VMEM((3, heads, tokens), F32)],
        ),
        out_shape=[
            pltpu.HBM((tokens, part * HEAD_DIM), F32),
            pltpu.HBM((tokens, part * HEAD_DIM), BF16),
            jax.ShapeDtypeStruct((part, HEAD_DIM, 2 * HEAD_DIM), BF16),
        ],
        compiler_params=pltpu.CompilerParams(vmem_limit_bytes=14 << 20),
        cost_estimate=pl.CostEstimate(flops=part * 1500000000, bytes_accessed=8 << 20, transcendentals=0),
        name="local",
    )(flags, queries, keys, values, log_decay, beta, weights)


def join(later, first):
    both = mm(later[:, HEAD_DIM:], first)
    return jnp.concatenate([both[:, :HEAD_DIM] + later[:, :HEAD_DIM].astype(F32), both[:, HEAD_DIM:]], axis=1)


def pair_kernel(bits, mine_ref, sib_ref, *outs):
    core = bits[0]
    chip = bits[1] + 2 * bits[2]

    def run(first, second):
        for d in range(CHIPS):
            h = CHIPS * core + (chip ^ d)
            outs[d][...] = join(second[h], first[h]).astype(BF16)

    @pl.when(core == 1)
    def _():
        run(sib_ref, mine_ref)

    @pl.when(core == 0)
    def _():
        run(mine_ref, sib_ref)


def group_kernel(bits, *refs):
    taken, (total_ref, *back_refs), (maps, backs) = refs[:CHIPS], refs[CHIPS:2 * CHIPS + 1], refs[2 * CHIPS + 1:]
    chip = bits[1] + 2 * bits[2]
    for d in range(CHIPS):
        maps[chip ^ d] = taken[d][...]
    row_i = lax.broadcasted_iota(jnp.int32, (HEAD_DIM, HEAD_DIM), 0)
    col_i = lax.broadcasted_iota(jnp.int32, (HEAD_DIM, HEAD_DIM), 1)
    eye = (row_i == col_i).astype(F32).astype(BF16)
    none = jnp.zeros((HEAD_DIM, HEAD_DIM), BF16)
    m0, m1, m2, m3 = (maps[i] for i in range(CHIPS))
    low = join(m1, m0).astype(BF16)
    high = join(m3, m2)
    both = mm(jnp.concatenate([m2[:, HEAD_DIM:], high[:, HEAD_DIM:].astype(BF16)], axis=0), low)
    third = both[:HEAD_DIM].astype(BF16)
    total_ref[:, :HEAD_DIM] = (both[HEAD_DIM:, :HEAD_DIM] + high[:, :HEAD_DIM]).astype(BF16)
    total_ref[:, HEAD_DIM:] = both[HEAD_DIM:, HEAD_DIM:].astype(BF16)
    backs[0] = jnp.concatenate([none, none, eye], axis=1)
    backs[1] = jnp.concatenate([m0[:, :HEAD_DIM], none, m0[:, HEAD_DIM:]], axis=1)
    backs[2] = jnp.concatenate([none, low], axis=1)
    backs[3] = jnp.concatenate([m2[:, :HEAD_DIM], third], axis=1)
    for d in range(CHIPS):
        back_refs[d][...] = backs[chip ^ d]


def near_kernel(bits, sib_ref, cur_ref, state_ref, x_ref, carry_ref):
    bit = bits[3]
    row_i = lax.broadcasted_iota(jnp.int32, (HEAD_DIM, HEAD_DIM), 0)
    col_i = lax.broadcasted_iota(jnp.int32, (HEAD_DIM, HEAD_DIM), 1)
    eye = (row_i == col_i).astype(F32).astype(BF16)
    sib, cur = sib_ref[...], cur_ref[...]
    upper = bit == 1
    first = jnp.where(upper, sib, cur)
    later = jnp.where(upper, cur, sib)
    state = mm(later[:, HEAD_DIM:], first[:, :HEAD_DIM]) + later[:, :HEAD_DIM].astype(F32)
    state_ref[...] = state.astype(BF16)
    x_ref[...] = jnp.where(upper, sib[:, :HEAD_DIM], jnp.zeros((HEAD_DIM, HEAD_DIM), BF16))
    carry_ref[...] = jnp.where(upper, sib[:, HEAD_DIM:], eye)


def top_kernel(bits, sib_ref, carried_ref, x_ref):
    x = mm(carried_ref[...], sib_ref[...])
    x_ref[...] = jnp.where(bits[4] == 1, x, 0.0).astype(BF16)


def small_call(kernel, bits, args, outs, scratch=()):
    return pl.pallas_call(
        kernel,
        grid_spec=pltpu.PrefetchScalarGridSpec(
            num_scalar_prefetch=1,
            grid=(1,),
            in_specs=[pl.BlockSpec(a.shape, lambda i, b, n=a.ndim: (0,) * n) for a in args],
            out_specs=[pl.BlockSpec(o.shape, lambda i, b, n=len(o.shape): (0,) * n) for o in outs],
            scratch_shapes=list(scratch),
        ),
        out_shape=outs,
        compiler_params=pltpu.CompilerParams(vmem_limit_bytes=3 << 20),
        cost_estimate=pl.CostEstimate(flops=600000000, bytes_accessed=1 << 20, transcendentals=0),
    )(bits, *args)


def final_kernel(base, bits, near_ref, far_ref, sib_ref, weight_ref, gain_ref, *refs):
    core = bits[0]
    chip = bits[1] + 2 * bits[2]
    backs, nexts, tops = refs[:GROUP], refs[GROUP:2 * GROUP], refs[2 * GROUP:3 * GROUP]
    z_ref, all_back, all_far = refs[-3:]
    tokens = near_ref.shape[0]
    step = pl.program_id(0)
    upper = core == 1
    first = LOCAL_LEVELS

    @pl.when(step == 0)
    def _():
        for k in range(GROUP):
            head = CHIPS * (core ^ (k & 1)) + (chip ^ (k >> 1))
            all_back[head] = backs[k][...]
            all_far[head, :, :HEAD_DIM] = nexts[k][...]
            all_far[head, :, HEAD_DIM:] = tops[k][...]

    def lanes(g):
        return slice(g * HEAD_DIM, (g + 1) * HEAD_DIM)

    heads = [TOGETHER * (base + step) + g for g in range(TOGETHER)]
    back = [all_back[h] for h in heads]
    outer = [mm(back[g][:, 2 * HEAD_DIM:], all_far[h]).astype(BF16) for g, h in enumerate(heads)]
    states = [jnp.concatenate([back[g][:, :2 * HEAD_DIM], outer[g]], axis=1) for g in range(TOGETHER)]
    moved = [mm(sib_ref[g, :, HEAD_DIM:], states[g]).astype(BF16) for g in range(TOGETHER)]
    stacks = []
    for g in range(TOGETHER):
        low = jnp.where(upper, sib_ref[g, :, :HEAD_DIM], jnp.zeros((HEAD_DIM, HEAD_DIM), BF16))
        stacks.append(jnp.transpose(jnp.concatenate([low, jnp.where(upper, moved[g], states[g])], axis=1)))
    levels = stacks[0].shape[0] // HEAD_DIM
    size = 2 * SUPER
    units = [(g, t) for g in range(TOGETHER) for t in range(0, tokens, size)]
    reads = [lax.dot_general(stacks[g], far_ref[t:t + size, lanes(g)],
                             (((1,), (1,)), ((), ())), preferred_element_type=F32) for g, t in units]
    for u, (g, t) in enumerate(units):
        turned = None
        for i in range(levels):
            row = weight_ref[first + i, pl.ds(heads[g], 1), t:t + size]
            term = row * reads[u][i * HEAD_DIM:(i + 1) * HEAD_DIM]
            turned = term if turned is None else turned + term
        y = near_ref[t:t + size, lanes(g)] + jnp.transpose(turned)
        scale = lax.rsqrt(jnp.mean(y * y, axis=1, keepdims=True) + EPS)
        z_ref[t:t + size, lanes(g)] = (y * scale * gain_ref[:, lanes(g)]).astype(BF16)


def final_part(base, steps, bits, near, far, sib, weights, gain, backs, nexts, tops, before=None):
    tokens, width = near.shape
    wide = TOGETHER * HEAD_DIM
    block = pl.BlockSpec((tokens, wide), lambda h, b: (0, base + h))

    def whole(a):
        return pl.BlockSpec(a.shape, lambda h, b, n=a.ndim: (0,) * n)

    rest = [*backs, *nexts, *tops]
    in_specs = [block, block, pl.BlockSpec((TOGETHER, HEAD_DIM, 2 * HEAD_DIM), lambda h, b: (base + h, 0, 0)),
                whole(weights), pl.BlockSpec((1, wide), lambda h, b: (0, base + h))] + [whole(a) for a in rest]
    args = [bits, near, far, sib, weights, gain, *rest]
    aliases = {}
    if before is not None:
        aliases = {len(args): 0}
        args.append(before)
        in_specs.append(pl.BlockSpec(memory_space=pl.ANY))
    return pl.pallas_call(
        functools.partial(final_kernel, base),
        grid_spec=pltpu.PrefetchScalarGridSpec(
            num_scalar_prefetch=1,
            grid=(steps,),
            in_specs=in_specs,
            out_specs=block,
            scratch_shapes=[pltpu.VMEM((GROUP, HEAD_DIM, 3 * HEAD_DIM), BF16),
                            pltpu.VMEM((GROUP, HEAD_DIM, 2 * HEAD_DIM), BF16)],
        ),
        out_shape=jax.ShapeDtypeStruct((tokens, width), BF16),
        input_output_aliases=aliases,
        compiler_params=pltpu.CompilerParams(vmem_limit_bytes=14 << 20),
        cost_estimate=pl.CostEstimate(flops=2400000000, bytes_accessed=4 << 20, transcendentals=0),
    )(*args)


def partner(value, mask):
    size = lax.axis_size("seq")
    return lax.ppermute(value, "seq", [(i, i ^ mask) for i in range(size)])


def order_pieces():
    return [p for i in range(PIECES) for p in (i, PIECES + i)]


def project(z, out_weight):
    size = lax.axis_size("head")
    me = lax.axis_index("head")
    rows = z.shape[0] // size
    cols = out_weight.shape[1] // (2 * PIECES)
    up = [(j, (j + 1) % size) for j in range(size)]
    down = [(j, (j - 1) % size) for j in range(size)]

    def term(block, piece):
        part = lax.dynamic_slice_in_dim(z, (block % size) * rows, rows, 0)
        w = out_weight[:, piece * cols:(piece + 1) * cols]
        return jnp.dot(part, w, preferred_element_type=F32).astype(BF16)

    order = order_pieces()
    sums = {}
    for p in order:
        sums[p] = term(me + size - 1 if p < PIECES else me + 1, p)
    last = None
    for s in range(size - 1):
        got, own = {}, {}
        for p in order:
            got[p] = lax.ppermute(sums[p], "head", up if p < PIECES else down)
            own[p] = term(me + 2 * size - 2 - s if p < PIECES else me + 2 + s, p)
        for p in order:
            keep = (own[p],) if last is None else (own[p], last)
            mine = lax.optimization_barrier(keep)[0]
            last = (got[p].astype(F32) + mine.astype(F32)).astype(BF16)
            sums[p] = last
    return jnp.concatenate([sums[p] for p in range(2 * PIECES)], axis=1)


def layer(queries, keys, values, log_decay, beta, level_weights, doc_start, norm_gain, out_weight):
    nbits = lax.axis_size("seq").bit_length() - 1
    index = lax.axis_index("seq")
    bits = jnp.stack([(index >> b) & 1 for b in range(nbits)]).astype(jnp.int32)
    in_hbm = lambda x: pltpu.with_memory_space_constraint(x, pltpu.HBM)
    given = [in_hbm(x) for x in (doc_start, queries, keys, values, log_decay, beta, level_weights)]
    wide = jax.ShapeDtypeStruct((HEAD_DIM, 2 * HEAD_DIM), BF16)
    square = jax.ShapeDtypeStruct((HEAD_DIM, HEAD_DIM), BF16)
    back = jax.ShapeDtypeStruct((HEAD_DIM, 3 * HEAD_DIM), BF16)
    near, far, maps = local_part(*given)
    sib = partner(maps, 1)
    sends = small_call(pair_kernel, bits, [maps, sib], [wide] * CHIPS)
    taken = [sends[0]] + [partner(sends[d], 2 * d) for d in range(1, CHIPS)]
    total, *outs = small_call(
        group_kernel, bits, taken, [wide] + [back] * CHIPS,
        [pltpu.VMEM((CHIPS, HEAD_DIM, 2 * HEAD_DIM), BF16), pltpu.VMEM((CHIPS, HEAD_DIM, 3 * HEAD_DIM), BF16)])
    got = partner(total, GROUP)
    state, x_near, carried = small_call(near_kernel, bits, [got, total], [square] * 3)
    got = partner(state, 2 * GROUP)
    x_top = small_call(top_kernel, bits, [got, carried], [square])[0]
    backs = []
    for d in range(CHIPS):
        mine = outs[d] if d == 0 else partner(outs[d], 2 * d)
        backs += [mine, partner(mine, 1)]
    nexts = [x_near] + [partner(x_near, k) for k in range(1, GROUP)]
    tops = [x_top] + [partner(x_top, k) for k in range(1, GROUP)]
    z = None
    for base in (0, 2):
        z = final_part(base, 2, bits, in_hbm(near), in_hbm(far), sib, given[6], norm_gain.reshape(1, -1),
                       backs, nexts, tops, z)
    return project(z, out_weight)


def solution(mesh):
    placed = (
        P("seq", "head"),
        P("seq", "head"),
        P("seq", "head"),
        P("head", "seq"),
        P("head", "seq"),
        P(None, "head", "seq"),
        P("seq"),
        P("head"),
        P("head", None),
    )
    return jax.shard_map(layer, mesh=mesh, in_specs=placed, out_specs=P(("seq", "head"), None), check_vma=False)
```

```python
import functools
import jax
import jax.numpy as jnp
from jax import lax
from jax.experimental import pallas as pl
from jax.experimental.pallas import tpu as pltpu
from jax.sharding import PartitionSpec as P


SPAN = 64
SUPER = 128
HEAD_DIM = 128
LOCAL_LEVELS = 4
TOGETHER = 2
CHUNKS = 2
TOP = 4
PIECES = 2
EPS = 1e-06
F32 = jnp.float32
BF16 = jnp.bfloat16


def mm(a, b):
    return jnp.dot(a, b, preferred_element_type=F32)


def local_kernel(flags, q_ref, k_ref, v_ref, log_ref, beta_ref, weight_ref,
                 near_ref, far_ref, map_ref, rows_ref):
    step = pl.program_id(0)
    tokens = q_ref.shape[0]
    heads = log_ref.shape[0]
    supers = tokens // SUPER
    spans = tokens // SPAN
    row_i = lax.broadcasted_iota(jnp.int32, (SUPER, SUPER), 0)
    col_i = lax.broadcasted_iota(jnp.int32, (SUPER, SUPER), 1)
    same = (row_i >> 6) == (col_i >> 6)
    lower = same & (row_i >= col_i)
    strict = same & (row_i > col_i)
    eye = (row_i == col_i).astype(F32)

    @pl.when(step == 0)
    def _():
        upto = (same & (row_i <= col_i)).astype(F32)
        both = jnp.concatenate([upto, strict.astype(F32)], axis=1)
        pieces = [
            jnp.dot(log_ref[:, s * SUPER:(s + 1) * SUPER], both,
                    precision=lax.Precision.HIGHEST, preferred_element_type=F32)
            for s in range(supers)
        ]
        cum = jnp.concatenate([p[:, :SUPER] for p in pieces], axis=1)
        tail = jnp.concatenate([p[:, SUPER:] for p in pieces], axis=1)
        span_i = lax.broadcasted_iota(jnp.int32, (heads, tokens), 1) >> 6
        keep = jnp.ones((heads, tokens), F32)
        for j in range(spans):
            keep = jnp.where(span_i == j, (1 - flags[j]).astype(F32), keep)
        rows_ref[0] = cum
        rows_ref[1] = jnp.exp(tail)
        rows_ref[2] = jnp.exp(cum) * keep

    units = [(g, s) for g in range(TOGETHER) for s in range(supers)]
    cols, cum_rows, tail_rows, beta_rows = [], [], [], []
    for g in range(TOGETHER):
        head = TOGETHER * step + g
        take = pl.ds(head, 1)
        beta_row = beta_ref[take, :]
        wanted = [rows_ref[0, take, :], rows_ref[2, take, :], beta_row]
        wanted += [weight_ref[level, take, :] for level in range(LOCAL_LEVELS)]
        wanted += [jnp.zeros((1, tokens), F32)]
        c = jnp.transpose(jnp.concatenate(wanted, axis=0))
        cols.append(c)
        cum_rows.append(rows_ref[0, take, :])
        tail_rows.append(rows_ref[1, take, :])
        beta_rows.append(beta_row)

    def cut(s):
        return slice(s * SUPER, (s + 1) * SUPER)

    def lanes(g):
        return slice(g * HEAD_DIM, (g + 1) * HEAD_DIM)

    def col(g, s, i):
        return cols[g][cut(s), i:i + 1]

    scores, powers, inverses, right, tails, queries = [], [], [], [], [], []
    for g, s in units:
        q = q_ref[cut(s), lanes(g)]
        k = k_ref[cut(s), lanes(g)]
        k_t = jnp.transpose(k)
        grams = mm(jnp.concatenate([q, k], axis=0), k_t)
        qf, kf, ktf = q.astype(F32), k.astype(F32), k_t.astype(F32)
        rq = lax.rsqrt(jnp.sum(qf * qf, axis=1, keepdims=True) + EPS)
        rk = lax.rsqrt(jnp.sum(kf * kf, axis=1, keepdims=True) + EPS)
        rk_row = lax.rsqrt(jnp.sum(ktf * ktf, axis=0, keepdims=True) + EPS)
        spread = col(g, s, 0) - cum_rows[g][:, cut(s)]
        ratio = jnp.exp(jnp.where(lower, spread, -1e30)) * rk_row
        scores.append((ratio * (rq * grams[:SUPER])).astype(BF16))
        power = jnp.where(strict, (-col(g, s, 2) * rk) * ratio * grams[SUPER:], 0.0)
        inverses.append(eye + power)
        powers.append(power.astype(BF16))
        decay = col(g, s, 1)
        right.append(jnp.concatenate([v_ref[cut(s), lanes(g)], (decay * rk * kf).astype(BF16)], axis=1))
        tails.append((ktf * (rk_row * tail_rows[g][:, cut(s)])).astype(BF16))
        queries.append(decay * rq * qf)

    n = len(units)
    powers = [mm(p, p).astype(BF16) for p in powers]
    for _ in range(4):
        both = [mm(powers[u], jnp.concatenate([powers[u], inverses[u].astype(BF16)], axis=1)) for u in range(n)]
        powers = [b[:, :SUPER].astype(BF16) for b in both]
        inverses = [inverses[u] + both[u][:, SUPER:] for u in range(n)]
    inverses = [inverses[u] + mm(powers[u], inverses[u].astype(BF16)) for u in range(n)]
    solved = []
    for u, (g, s) in enumerate(units):
        scaled = (inverses[u] * beta_rows[g][:, cut(s)]).astype(BF16)
        solved.append(mm(scaled, right[u]).astype(BF16))
    leaves = [[] for _ in range(TOGETHER)]
    for u, (g, s) in enumerate(units):
        for half in range(SUPER // SPAN):
            a, b = half * SPAN, (half + 1) * SPAN
            summary = mm(tails[u][:, a:b], solved[u][a:b, :])
            t = s * SUPER + b - 1
            last = jnp.broadcast_to(cols[g][t:t + 1, 1:2], (1, HEAD_DIM))
            leaves[g].append((summary[:, :HEAD_DIM], summary[:, HEAD_DIM:], last))
    outs = [[] for _ in range(TOGETHER)]
    readers = [[] for _ in range(TOGETHER)]
    for u, (g, s) in enumerate(units):
        read = mm(scores[u], solved[u])
        out = col(g, s, 3) * read[:, :HEAD_DIM]
        reader = queries[u] - read[:, HEAD_DIM:]
        for half in range(SUPER // SPAN):
            a, b = half * SPAN, (half + 1) * SPAN
            outs[g].append(out[a:b])
            readers[g].append(reader[a:b])

    for level in range(1, LOCAL_LEVELS):
        for g in range(TOGETHER):
            maps = leaves[g]
            new_outs, new_readers, new_maps = [], [], []
            for i in range(0, len(maps), 2):
                (s_lo, e_lo, d_lo), (s_hi, e_hi, d_hi) = maps[i], maps[i + 1]
                r_hi = readers[g][i + 1]
                m = r_hi.shape[0]
                t0 = (i + 1) * m
                w_c = cols[g][t0:t0 + m, 3 + level:4 + level]
                both = mm(jnp.concatenate([r_hi.astype(BF16), e_hi.astype(BF16)], axis=0),
                          jnp.concatenate([s_lo.astype(BF16), e_lo.astype(BF16)], axis=1))
                new_outs.append(jnp.concatenate(
                    [outs[g][i], outs[g][i + 1] + w_c * both[:m, :HEAD_DIM]], axis=0))
                new_readers.append(jnp.concatenate(
                    [readers[g][i], d_lo * r_hi - both[:m, HEAD_DIM:]], axis=0))
                new_maps.append((d_hi * s_lo + s_hi - both[m:, :HEAD_DIM],
                                 d_hi * e_lo + d_lo * e_hi - both[m:, HEAD_DIM:],
                                 d_lo * d_hi))
            outs[g], readers[g], leaves[g] = new_outs, new_readers, new_maps
    for g in range(TOGETHER):
        total, erase, decay = leaves[g][0]
        near_ref[:, lanes(g)] = outs[g][0]
        far_ref[:, lanes(g)] = readers[g][0].astype(BF16)
        map_ref[g] = jnp.concatenate([total, eye * decay - erase], axis=1).astype(BF16)


def local_part(flags, queries, keys, values, log_decay, beta, weights):
    tokens = queries.shape[0]
    heads = log_decay.shape[0]
    wide = TOGETHER * HEAD_DIM
    steps = heads // TOGETHER
    block = pl.BlockSpec((tokens, wide), lambda h, f: (0, h))
    out = block
    whole2 = pl.BlockSpec((heads, tokens), lambda h, f: (0, 0))
    whole3 = pl.BlockSpec(weights.shape, lambda h, f: (0, 0, 0))
    part = steps * TOGETHER
    return pl.pallas_call(
        local_kernel,
        grid_spec=pltpu.PrefetchScalarGridSpec(
            num_scalar_prefetch=1,
            grid=(steps,),
            in_specs=[block, block, block, whole2, whole2, whole3],
            out_specs=[out, out,
                       pl.BlockSpec((TOGETHER, HEAD_DIM, 2 * HEAD_DIM), lambda h, f: (h, 0, 0))],
            scratch_shapes=[pltpu.VMEM((3, heads, tokens), F32)],
        ),
        out_shape=[
            pltpu.HBM((tokens, part * HEAD_DIM), F32),
            pltpu.HBM((tokens, part * HEAD_DIM), BF16),
            jax.ShapeDtypeStruct((part, HEAD_DIM, 2 * HEAD_DIM), BF16),
        ],
        compiler_params=pltpu.CompilerParams(vmem_limit_bytes=14 << 20),
        cost_estimate=pl.CostEstimate(flops=part * 1500000000, bytes_accessed=8 << 20, transcendentals=0),
        name="local",
    )(flags, queries, keys, values, log_decay, beta, weights)


def pair_kernel(bits, mine_ref, sib_ref, *outs):
    core = bits[0]
    half = outs[0].shape[0]

    def run(first, second):
        for c, cur_ref in enumerate(outs):
            for g in range(half):
                h = half * (len(outs) * core + c) + g
                later = second[h]
                both = mm(later[:, HEAD_DIM:], first[h])
                cur_ref[g, :, :HEAD_DIM] = (both[:, :HEAD_DIM] + later[:, :HEAD_DIM].astype(F32)).astype(BF16)
                cur_ref[g, :, HEAD_DIM:] = both[:, HEAD_DIM:].astype(BF16)

    @pl.when(core == 1)
    def _():
        run(sib_ref, mine_ref)

    @pl.when(core == 0)
    def _():
        run(mine_ref, sib_ref)


def level_kernel(level, packs, bits, *refs):
    refs = list(refs)
    if packs:
        gathered = refs[:2 * (TOP - 1) - 1]
        refs, pack = refs[len(gathered):-1], refs[-1]
    if level == 1:
        sib_ref, cur_ref, new_ref, x_ref, carry_ref = refs
    else:
        sib_ref, cur_ref, carried_ref, new_ref, x_ref, carry_ref = refs
    bit = bits[level]
    half = cur_ref.shape[0]

    def store(g, both, later):
        new_ref[g, :, :HEAD_DIM] = (both[:, :HEAD_DIM] + later[:, :HEAD_DIM].astype(F32)).astype(BF16)
        new_ref[g, :, HEAD_DIM:] = both[:, HEAD_DIM:].astype(BF16)

    @pl.when(bit == 1)
    def _():
        for g in range(half):
            later, sib = cur_ref[g], sib_ref[g]
            if level == 1:
                store(g, mm(later[:, HEAD_DIM:], sib), later)
                x_ref[g] = sib[:, :HEAD_DIM]
                carry_ref[g] = sib[:, HEAD_DIM:]
            else:
                both = mm(jnp.concatenate([later[:, HEAD_DIM:], carried_ref[g]], axis=0), sib)
                store(g, both[:HEAD_DIM], later)
                x_ref[g] = both[HEAD_DIM:, :HEAD_DIM].astype(BF16)
                carry_ref[g] = both[HEAD_DIM:, HEAD_DIM:].astype(BF16)

    @pl.when(bit == 0)
    def _():
        row_i = lax.broadcasted_iota(jnp.int32, (HEAD_DIM, HEAD_DIM), 0)
        col_i = lax.broadcasted_iota(jnp.int32, (HEAD_DIM, HEAD_DIM), 1)
        eye = (row_i == col_i).astype(F32).astype(BF16)
        for g in range(half):
            later = sib_ref[g]
            store(g, mm(later[:, HEAD_DIM:], cur_ref[g]), later)
            x_ref[g] = jnp.zeros((HEAD_DIM, HEAD_DIM), BF16)
            carry_ref[g] = eye if level == 1 else carried_ref[g]

    if packs:
        for i, source in enumerate([*gathered, x_ref]):
            for g in range(half):
                pack[i * half + g] = source[g]


def top_kernel(bits, *refs):
    x_ref = refs[-1]
    half = x_ref.shape[0] // CHUNKS

    @pl.when(bits[TOP] == 1)
    def _():
        for c in range(CHUNKS):
            for g in range(half):
                x_ref[c * half + g] = mm(refs[CHUNKS + c][g], refs[c][g]).astype(BF16)

    @pl.when(bits[TOP] == 0)
    def _():
        x_ref[...] = jnp.zeros(x_ref.shape, BF16)


def state_kernel(bits, sib_ref, mine_ref, other_ref, mine_top, other_top, stack_ref):
    core = bits[0]
    upper = core == 1
    heads = sib_ref.shape[0]
    half = heads // 2
    per = half // CHUNKS
    for h in range(heads):
        is_mine = core == h // half
        j = h % half
        rows = [(j // per) * (TOP - 1) * per + level * per + j % per for level in range(TOP - 1)]
        parts = [jnp.where(is_mine, mine_ref[r], other_ref[r]) for r in rows]
        parts.append(jnp.where(is_mine, mine_top[j], other_top[j]))
        states = jnp.concatenate(parts, axis=1)
        moved = mm(sib_ref[h, :, HEAD_DIM:], states).astype(BF16)
        low = jnp.where(upper, sib_ref[h, :, :HEAD_DIM], jnp.zeros((HEAD_DIM, HEAD_DIM), BF16))
        stack_ref[h] = jnp.transpose(jnp.concatenate([low, jnp.where(upper, moved, states)], axis=1))


def small_call(kernel, bits, args, outs, scratch=()):
    return pl.pallas_call(
        kernel,
        grid_spec=pltpu.PrefetchScalarGridSpec(
            num_scalar_prefetch=1,
            grid=(1,),
            in_specs=[pl.BlockSpec(a.shape, lambda i, b, n=a.ndim: (0,) * n) for a in args],
            out_specs=[pl.BlockSpec(o.shape, lambda i, b, n=len(o.shape): (0,) * n) for o in outs],
            scratch_shapes=list(scratch),
        ),
        out_shape=outs,
        compiler_params=pltpu.CompilerParams(vmem_limit_bytes=8 << 20),
        cost_estimate=pl.CostEstimate(flops=600000000, bytes_accessed=1 << 20, transcendentals=0),
    )(bits, *args)


def read_kernel(bits, near_a, near_b, far_a, far_b, weight_a, weight_b, stack_ref, gain_ref, z_ref):
    step = pl.program_id(0)
    levels = stack_ref.shape[1] // HEAD_DIM

    def lanes(g):
        return slice(g * HEAD_DIM, (g + 1) * HEAD_DIM)

    count = range(gain_ref.shape[1] // HEAD_DIM)
    reads = [lax.dot_general(stack_ref[g], jnp.concatenate([far_a[:, lanes(g)], far_b[:, lanes(g)]], axis=0),
                             (((1,), (1,)), ((), ())), preferred_element_type=F32) for g in count]
    for g in count:
        head = pl.ds(len(count) * step + g, 1)
        turned = None
        for i in range(levels):
            row = jnp.concatenate([weight_a[LOCAL_LEVELS + i, head, :], weight_b[LOCAL_LEVELS + i, head, :]], axis=1)
            term = row * reads[g][i * HEAD_DIM:(i + 1) * HEAD_DIM]
            turned = term if turned is None else turned + term
        y = jnp.concatenate([near_a[:, lanes(g)], near_b[:, lanes(g)]], axis=0) + jnp.transpose(turned)
        scale = lax.rsqrt(jnp.mean(y * y, axis=1, keepdims=True) + EPS)
        z_ref[:, lanes(g)] = (y * scale * gain_ref[:, lanes(g)]).astype(BF16)


def read_part(offsets, blocks, bits, near, far, weights, stacks, gain):
    tokens, width = near.shape
    rows = tokens // blocks
    heads = stacks.shape[0] // 2
    wide = heads * HEAD_DIM
    place = bits.shape[0] - 1

    def token_block(offset):
        return pl.BlockSpec((rows, wide), lambda h, b: ((b[place] + offset) & (blocks - 1), h))

    def weight_block(offset):
        return pl.BlockSpec((*weights.shape[:2], rows), lambda h, b: (0, 0, (b[place] + offset) & (blocks - 1)))

    return pl.pallas_call(
        read_kernel,
        grid_spec=pltpu.PrefetchScalarGridSpec(
            num_scalar_prefetch=1,
            grid=(2,),
            in_specs=[token_block(o) for o in offsets] * 2 + [weight_block(o) for o in offsets]
                     + [pl.BlockSpec((heads, *stacks.shape[1:]), lambda h, b: (h, 0, 0)),
                        pl.BlockSpec((1, wide), lambda h, b: (0, h))],
            out_specs=pl.BlockSpec((2 * rows, wide), lambda h, b: (0, h)),
        ),
        out_shape=jax.ShapeDtypeStruct((2 * rows, width), BF16),
        compiler_params=pltpu.CompilerParams(vmem_limit_bytes=14 << 20),
        cost_estimate=pl.CostEstimate(flops=2400000000, bytes_accessed=4 << 20, transcendentals=0),
    )(bits, near, near, far, far, weights, weights, stacks, gain)


def partner(value, mask):
    size = lax.axis_size("seq")
    return lax.ppermute(value, "seq", [(i, i ^ mask) for i in range(size)])


def order_pieces():
    return [p for i in range(PIECES) for p in (i, PIECES + i)]


def project(first_rows, make_last, out_weight):
    size = lax.axis_size("head")
    rows = first_rows.shape[0] // 2
    cols = out_weight.shape[1] // (2 * PIECES)
    ring = [[(j, (j + 1) % size) for j in range(size)], [(j, (j - 1) % size) for j in range(size)]]

    def term(block, piece):
        w = out_weight[:, piece * cols:(piece + 1) * cols]
        return jnp.dot(block, w, preferred_element_type=F32).astype(BF16)

    order = order_pieces()
    before, after = first_rows[:rows], first_rows[rows:]
    sums = {}
    for p in order:
        sums[p] = term(before if p < PIECES else after, p)
    last_rows = make_last()
    across, own_rows = last_rows[:rows], last_rows[rows:]
    sources = [(across, across), (after, before), (own_rows, own_rows)]
    last = None
    for s in range(size - 1):
        got, own = {}, {}
        for p in order:
            side = int(p >= PIECES)
            got[p] = lax.ppermute(sums[p], "head", ring[side])
            own[p] = term(sources[s][side], p)
        for p in order:
            keep = (own[p],) if last is None else (own[p], last)
            mine = lax.optimization_barrier(keep)[0]
            last = (got[p].astype(F32) + mine.astype(F32)).astype(BF16)
            sums[p] = last
    return jnp.concatenate([sums[p] for p in range(2 * PIECES)], axis=1)


def layer(queries, keys, values, log_decay, beta, level_weights, doc_start, norm_gain, out_weight):
    nbits = lax.axis_size("seq").bit_length() - 1
    blocks = lax.axis_size("head")
    index = lax.axis_index("seq")
    place = lax.axis_index("head")
    bits = jnp.stack([(index >> b) & 1 for b in range(nbits)] + [place]).astype(jnp.int32)
    gain = norm_gain.reshape(1, -1)
    in_hbm = lambda x: pltpu.with_memory_space_constraint(x, pltpu.HBM)
    given = [in_hbm(x) for x in (doc_start, queries, keys, values, log_decay, beta, level_weights)]
    heads = log_decay.shape[0]
    per = heads // (2 * CHUNKS)
    wide = jax.ShapeDtypeStruct((per, HEAD_DIM, 2 * HEAD_DIM), BF16)
    square = jax.ShapeDtypeStruct((per, HEAD_DIM, HEAD_DIM), BF16)
    near, far, maps = local_part(*given)
    sib = partner(maps, 1)
    curs = list(small_call(pair_kernel, bits, [maps, sib], [wide] * CHUNKS))
    carried = [None] * CHUNKS
    found = [[] for _ in range(CHUNKS)]
    packed = None
    for level in range(1, TOP):
        for c in range(CHUNKS):
            got = partner(curs[c], 1 << level)
            args = [got, curs[c]] if level == 1 else [got, curs[c], carried[c]]
            outs = [wide, square, square]
            packs = level == TOP - 1 and c == CHUNKS - 1
            if packs:
                args = [*found[0], *found[1], *args]
                outs = outs + [jax.ShapeDtypeStruct((CHUNKS * (TOP - 1) * per, HEAD_DIM, HEAD_DIM), BF16)]
            curs[c], x, carried[c], *packed = small_call(
                functools.partial(level_kernel, level, packs), bits, args, outs)
            found[c].append(x)
    got = [partner(curs[c][:, :, :HEAD_DIM], 1 << TOP) for c in range(CHUNKS)]
    top = small_call(top_kernel, bits, [*got, *carried],
                     [jax.ShapeDtypeStruct((CHUNKS * per, HEAD_DIM, HEAD_DIM), BF16)])[0]
    stacks = small_call(
        state_kernel, bits,
        [sib, packed[0], partner(packed[0], 1), top, partner(top, 1)],
        [jax.ShapeDtypeStruct((heads, (TOP + 1) * HEAD_DIM, HEAD_DIM), BF16)])[0]
    near, far = in_hbm(near), in_hbm(far)

    def read(offsets):
        return read_part(offsets, blocks, bits, near, far, given[6], stacks, gain)

    return project(read((blocks - 1, 1)), lambda: read((2, 0)), out_weight)


def solution(mesh):
    placed = (
        P("seq", "head"),
        P("seq", "head"),
        P("seq", "head"),
        P("head", "seq"),
        P("head", "seq"),
        P(None, "head", "seq"),
        P("seq"),
        P("head"),
        P("head", None),
    )
    return jax.shard_map(layer, mesh=mesh, in_specs=placed, out_specs=P(("seq", "head"), None), check_vma=False)
```

```python
import functools
import jax
import jax.numpy as jnp
from jax import lax
from jax.experimental import pallas as pl
from jax.experimental.pallas import tpu as pltpu
from jax.sharding import PartitionSpec as P


SPAN = 64
SUPER = 128
HEAD_DIM = 128
LOCAL_LEVELS = 4
TOGETHER = 2
CHUNKS = 2
TOP = 4
PIECES = 2
EPS = 1e-06
F32 = jnp.float32
BF16 = jnp.bfloat16


def mm(a, b):
    return jnp.dot(a, b, preferred_element_type=F32)


def local_kernel(flags, q_ref, k_ref, v_ref, log_ref, beta_ref, weight_ref,
                 near_ref, far_ref, map_ref, rows_ref):
    step = pl.program_id(0)
    tokens = q_ref.shape[0]
    heads = log_ref.shape[0]
    supers = tokens // SUPER
    spans = tokens // SPAN
    row_i = lax.broadcasted_iota(jnp.int32, (SUPER, SUPER), 0)
    col_i = lax.broadcasted_iota(jnp.int32, (SUPER, SUPER), 1)
    same = (row_i >> 6) == (col_i >> 6)
    lower = same & (row_i >= col_i)
    strict = same & (row_i > col_i)
    eye = (row_i == col_i).astype(F32)

    @pl.when(step == 0)
    def _():
        upto = (same & (row_i <= col_i)).astype(F32)
        both = jnp.concatenate([upto, strict.astype(F32)], axis=1)
        pieces = [
            jnp.dot(log_ref[:, s * SUPER:(s + 1) * SUPER], both,
                    precision=lax.Precision.HIGHEST, preferred_element_type=F32)
            for s in range(supers)
        ]
        cum = jnp.concatenate([p[:, :SUPER] for p in pieces], axis=1)
        tail = jnp.concatenate([p[:, SUPER:] for p in pieces], axis=1)
        span_i = lax.broadcasted_iota(jnp.int32, (heads, tokens), 1) >> 6
        keep = jnp.ones((heads, tokens), F32)
        for j in range(spans):
            keep = jnp.where(span_i == j, (1 - flags[j]).astype(F32), keep)
        rows_ref[0] = cum
        rows_ref[1] = jnp.exp(tail)
        rows_ref[2] = jnp.exp(cum) * keep

    units = [(g, s) for g in range(TOGETHER) for s in range(supers)]
    cols, cum_rows, tail_rows, beta_rows = [], [], [], []
    for g in range(TOGETHER):
        head = TOGETHER * step + g
        take = pl.ds(head, 1)
        beta_row = beta_ref[take, :]
        wanted = [rows_ref[0, take, :], rows_ref[2, take, :], beta_row]
        wanted += [weight_ref[level, take, :] for level in range(LOCAL_LEVELS)]
        wanted += [jnp.zeros((1, tokens), F32)]
        c = jnp.transpose(jnp.concatenate(wanted, axis=0))
        cols.append(c)
        cum_rows.append(rows_ref[0, take, :])
        tail_rows.append(rows_ref[1, take, :])
        beta_rows.append(beta_row)

    def cut(s):
        return slice(s * SUPER, (s + 1) * SUPER)

    def lanes(g):
        return slice(g * HEAD_DIM, (g + 1) * HEAD_DIM)

    def col(g, s, i):
        return cols[g][cut(s), i:i + 1]

    scores, powers, inverses, right, tails, queries = [], [], [], [], [], []
    for g, s in units:
        q = q_ref[cut(s), lanes(g)]
        k = k_ref[cut(s), lanes(g)]
        k_t = jnp.transpose(k)
        grams = mm(jnp.concatenate([q, k], axis=0), k_t)
        qf, kf, ktf = q.astype(F32), k.astype(F32), k_t.astype(F32)
        rq = lax.rsqrt(jnp.sum(qf * qf, axis=1, keepdims=True) + EPS)
        rk = lax.rsqrt(jnp.sum(kf * kf, axis=1, keepdims=True) + EPS)
        rk_row = lax.rsqrt(jnp.sum(ktf * ktf, axis=0, keepdims=True) + EPS)
        level = jnp.broadcast_to(col(g, s, 0), (SUPER, SUPER))
        spread = level - cum_rows[g][:, cut(s)]
        ratio = jnp.exp(jnp.where(lower, spread, -1e30)) * rk_row
        scores.append((ratio * (rq * grams[:SUPER])).astype(BF16))
        power = jnp.where(strict, (-col(g, s, 2) * rk) * ratio * grams[SUPER:], 0.0)
        inverses.append(eye + power)
        powers.append(power.astype(BF16))
        kept = [(1 - flags[s * (SUPER // SPAN) + i]).astype(F32) for i in range(SUPER // SPAN)]
        decay = jnp.exp(level) * jnp.where(row_i < SPAN, kept[0], kept[1])
        right.append(jnp.concatenate([v_ref[cut(s), lanes(g)], (decay * rk * kf).astype(BF16)], axis=1))
        tails.append((ktf * (rk_row * tail_rows[g][:, cut(s)])).astype(BF16))
        queries.append(decay * rq * qf)

    n = len(units)
    powers = [mm(p, p).astype(BF16) for p in powers]
    for _ in range(4):
        both = [mm(powers[u], jnp.concatenate([powers[u], inverses[u].astype(BF16)], axis=1)) for u in range(n)]
        powers = [b[:, :SUPER].astype(BF16) for b in both]
        inverses = [inverses[u] + both[u][:, SUPER:] for u in range(n)]
    inverses = [inverses[u] + mm(powers[u], inverses[u].astype(BF16)) for u in range(n)]
    solved = []
    for u, (g, s) in enumerate(units):
        scaled = (inverses[u] * beta_rows[g][:, cut(s)]).astype(BF16)
        solved.append(mm(scaled, right[u]).astype(BF16))
    leaves = [[] for _ in range(TOGETHER)]
    for u, (g, s) in enumerate(units):
        for half in range(SUPER // SPAN):
            a, b = half * SPAN, (half + 1) * SPAN
            summary = mm(tails[u][:, a:b], solved[u][a:b, :])
            t = s * SUPER + b - 1
            last = jnp.broadcast_to(cols[g][t:t + 1, 1:2], (1, HEAD_DIM))
            leaves[g].append((summary[:, :HEAD_DIM], summary[:, HEAD_DIM:], last))
    outs = [[] for _ in range(TOGETHER)]
    readers = [[] for _ in range(TOGETHER)]
    for u, (g, s) in enumerate(units):
        read = mm(scores[u], solved[u])
        out = col(g, s, 3) * read[:, :HEAD_DIM]
        reader = queries[u] - read[:, HEAD_DIM:]
        for half in range(SUPER // SPAN):
            a, b = half * SPAN, (half + 1) * SPAN
            outs[g].append(out[a:b])
            readers[g].append(reader[a:b])

    for level in range(1, LOCAL_LEVELS):
        for g in range(TOGETHER):
            maps = leaves[g]
            new_outs, new_readers, new_maps = [], [], []
            for i in range(0, len(maps), 2):
                (s_lo, e_lo, d_lo), (s_hi, e_hi, d_hi) = maps[i], maps[i + 1]
                r_hi = readers[g][i + 1]
                m = r_hi.shape[0]
                t0 = (i + 1) * m
                w_c = cols[g][t0:t0 + m, 3 + level:4 + level]
                both = mm(jnp.concatenate([r_hi.astype(BF16), e_hi.astype(BF16)], axis=0),
                          jnp.concatenate([s_lo.astype(BF16), e_lo.astype(BF16)], axis=1))
                new_outs.append(jnp.concatenate(
                    [outs[g][i], outs[g][i + 1] + w_c * both[:m, :HEAD_DIM]], axis=0))
                new_readers.append(jnp.concatenate(
                    [readers[g][i], d_lo * r_hi - both[:m, HEAD_DIM:]], axis=0))
                new_maps.append((d_hi * s_lo + s_hi - both[m:, :HEAD_DIM],
                                 d_hi * e_lo + d_lo * e_hi - both[m:, HEAD_DIM:],
                                 d_lo * d_hi))
            outs[g], readers[g], leaves[g] = new_outs, new_readers, new_maps
    for g in range(TOGETHER):
        total, erase, decay = leaves[g][0]
        near_ref[:, lanes(g)] = outs[g][0]
        far_ref[:, lanes(g)] = readers[g][0].astype(BF16)
        map_ref[g] = jnp.concatenate([total, eye * decay - erase], axis=1).astype(BF16)


def local_part(flags, queries, keys, values, log_decay, beta, weights):
    tokens = queries.shape[0]
    heads = log_decay.shape[0]
    wide = TOGETHER * HEAD_DIM
    steps = heads // TOGETHER
    block = pl.BlockSpec((tokens, wide), lambda h, f: (0, h))
    out = block
    whole2 = pl.BlockSpec((heads, tokens), lambda h, f: (0, 0))
    whole3 = pl.BlockSpec(weights.shape, lambda h, f: (0, 0, 0))
    part = steps * TOGETHER
    return pl.pallas_call(
        local_kernel,
        grid_spec=pltpu.PrefetchScalarGridSpec(
            num_scalar_prefetch=1,
            grid=(steps,),
            in_specs=[block, block, block, whole2, whole2, whole3],
            out_specs=[out, out,
                       pl.BlockSpec((TOGETHER, HEAD_DIM, 2 * HEAD_DIM), lambda h, f: (h, 0, 0))],
            scratch_shapes=[pltpu.VMEM((3, heads, tokens), F32)],
        ),
        out_shape=[
            pltpu.HBM((tokens, part * HEAD_DIM), F32),
            pltpu.HBM((tokens, part * HEAD_DIM), BF16),
            jax.ShapeDtypeStruct((part, HEAD_DIM, 2 * HEAD_DIM), BF16),
        ],
        compiler_params=pltpu.CompilerParams(vmem_limit_bytes=14 << 20),
        cost_estimate=pl.CostEstimate(flops=part * 1500000000, bytes_accessed=8 << 20, transcendentals=0),
        name="local",
    )(flags, queries, keys, values, log_decay, beta, weights)


def pair_kernel(bits, mine_ref, sib_ref, *outs):
    core = bits[0]
    half = outs[0].shape[0]

    def run(first, second):
        for c, cur_ref in enumerate(outs):
            for g in range(half):
                h = half * (len(outs) * core + c) + g
                later = second[h]
                both = mm(later[:, HEAD_DIM:], first[h])
                cur_ref[g, :, :HEAD_DIM] = (both[:, :HEAD_DIM] + later[:, :HEAD_DIM].astype(F32)).astype(BF16)
                cur_ref[g, :, HEAD_DIM:] = both[:, HEAD_DIM:].astype(BF16)

    @pl.when(core == 1)
    def _():
        run(sib_ref, mine_ref)

    @pl.when(core == 0)
    def _():
        run(mine_ref, sib_ref)


def level_kernel(level, packs, bits, *refs):
    refs = list(refs)
    if packs:
        gathered = refs[:2 * (TOP - 1) - 1]
        refs, pack = refs[len(gathered):-1], refs[-1]
    if level == 1:
        sib_ref, cur_ref, new_ref, x_ref, carry_ref = refs
    else:
        sib_ref, cur_ref, carried_ref, new_ref, x_ref, carry_ref = refs
    bit = bits[level]
    half = cur_ref.shape[0]

    def store(g, both, later):
        new_ref[g, :, :HEAD_DIM] = (both[:, :HEAD_DIM] + later[:, :HEAD_DIM].astype(F32)).astype(BF16)
        new_ref[g, :, HEAD_DIM:] = both[:, HEAD_DIM:].astype(BF16)

    @pl.when(bit == 1)
    def _():
        for g in range(half):
            later, sib = cur_ref[g], sib_ref[g]
            if level == 1:
                store(g, mm(later[:, HEAD_DIM:], sib), later)
                x_ref[g] = sib[:, :HEAD_DIM]
                carry_ref[g] = sib[:, HEAD_DIM:]
            else:
                both = mm(jnp.concatenate([later[:, HEAD_DIM:], carried_ref[g]], axis=0), sib)
                store(g, both[:HEAD_DIM], later)
                x_ref[g] = both[HEAD_DIM:, :HEAD_DIM].astype(BF16)
                carry_ref[g] = both[HEAD_DIM:, HEAD_DIM:].astype(BF16)

    @pl.when(bit == 0)
    def _():
        row_i = lax.broadcasted_iota(jnp.int32, (HEAD_DIM, HEAD_DIM), 0)
        col_i = lax.broadcasted_iota(jnp.int32, (HEAD_DIM, HEAD_DIM), 1)
        eye = (row_i == col_i).astype(F32).astype(BF16)
        for g in range(half):
            later = sib_ref[g]
            store(g, mm(later[:, HEAD_DIM:], cur_ref[g]), later)
            x_ref[g] = jnp.zeros((HEAD_DIM, HEAD_DIM), BF16)
            carry_ref[g] = eye if level == 1 else carried_ref[g]

    if packs:
        for i, source in enumerate([*gathered, x_ref]):
            for g in range(half):
                pack[i * half + g] = source[g]


def top_kernel(bits, *refs):
    x_ref = refs[-1]
    half = x_ref.shape[0] // CHUNKS

    @pl.when(bits[TOP] == 1)
    def _():
        for c in range(CHUNKS):
            for g in range(half):
                x_ref[c * half + g] = mm(refs[CHUNKS + c][g], refs[c][g]).astype(BF16)

    @pl.when(bits[TOP] == 0)
    def _():
        x_ref[...] = jnp.zeros(x_ref.shape, BF16)


def state_kernel(bits, sib_ref, mine_ref, other_ref, mine_top, other_top, stack_ref):
    core = bits[0]
    upper = core == 1
    heads = sib_ref.shape[0]
    half = heads // 2
    per = half // CHUNKS
    for h in range(heads):
        is_mine = core == h // half
        j = h % half
        rows = [(j // per) * (TOP - 1) * per + level * per + j % per for level in range(TOP - 1)]
        parts = [jnp.where(is_mine, mine_ref[r], other_ref[r]) for r in rows]
        parts.append(jnp.where(is_mine, mine_top[j], other_top[j]))
        states = jnp.concatenate(parts, axis=1)
        moved = mm(sib_ref[h, :, HEAD_DIM:], states).astype(BF16)
        low = jnp.where(upper, sib_ref[h, :, :HEAD_DIM], jnp.zeros((HEAD_DIM, HEAD_DIM), BF16))
        stack_ref[h] = jnp.transpose(jnp.concatenate([low, jnp.where(upper, moved, states)], axis=1))


def small_call(kernel, bits, args, outs, scratch=()):
    return pl.pallas_call(
        kernel,
        grid_spec=pltpu.PrefetchScalarGridSpec(
            num_scalar_prefetch=1,
            grid=(1,),
            in_specs=[pl.BlockSpec(a.shape, lambda i, b, n=a.ndim: (0,) * n) for a in args],
            out_specs=[pl.BlockSpec(o.shape, lambda i, b, n=len(o.shape): (0,) * n) for o in outs],
            scratch_shapes=list(scratch),
        ),
        out_shape=outs,
        compiler_params=pltpu.CompilerParams(vmem_limit_bytes=8 << 20),
        cost_estimate=pl.CostEstimate(flops=600000000, bytes_accessed=1 << 20, transcendentals=0),
    )(bits, *args)


def read_kernel(bits, near_a, near_b, far_a, far_b, weight_a, weight_b, stack_ref, gain_ref, z_ref):
    step = pl.program_id(0)
    levels = stack_ref.shape[1] // HEAD_DIM

    def lanes(g):
        return slice(g * HEAD_DIM, (g + 1) * HEAD_DIM)

    count = range(gain_ref.shape[1] // HEAD_DIM)
    reads = [lax.dot_general(stack_ref[g], jnp.concatenate([far_a[:, lanes(g)], far_b[:, lanes(g)]], axis=0),
                             (((1,), (1,)), ((), ())), preferred_element_type=F32) for g in count]
    for g in count:
        head = pl.ds(len(count) * step + g, 1)
        turned = None
        for i in range(levels):
            row = jnp.concatenate([weight_a[LOCAL_LEVELS + i, head, :], weight_b[LOCAL_LEVELS + i, head, :]], axis=1)
            term = row * reads[g][i * HEAD_DIM:(i + 1) * HEAD_DIM]
            turned = term if turned is None else turned + term
        y = jnp.concatenate([near_a[:, lanes(g)], near_b[:, lanes(g)]], axis=0) + jnp.transpose(turned)
        scale = lax.rsqrt(jnp.mean(y * y, axis=1, keepdims=True) + EPS)
        z_ref[:, lanes(g)] = (y * scale * gain_ref[:, lanes(g)]).astype(BF16)


def read_part(offsets, blocks, bits, near, far, weights, stacks, gain):
    tokens, width = near.shape
    rows = tokens // blocks
    heads = stacks.shape[0] // 2
    wide = heads * HEAD_DIM
    place = bits.shape[0] - 1

    def token_block(offset):
        return pl.BlockSpec((rows, wide), lambda h, b: ((b[place] + offset) & (blocks - 1), h))

    def weight_block(offset):
        return pl.BlockSpec((*weights.shape[:2], rows), lambda h, b: (0, 0, (b[place] + offset) & (blocks - 1)))

    return pl.pallas_call(
        read_kernel,
        grid_spec=pltpu.PrefetchScalarGridSpec(
            num_scalar_prefetch=1,
            grid=(2,),
            in_specs=[token_block(o) for o in offsets] * 2 + [weight_block(o) for o in offsets]
                     + [pl.BlockSpec((heads, *stacks.shape[1:]), lambda h, b: (h, 0, 0)),
                        pl.BlockSpec((1, wide), lambda h, b: (0, h))],
            out_specs=pl.BlockSpec((2 * rows, wide), lambda h, b: (0, h)),
        ),
        out_shape=jax.ShapeDtypeStruct((2 * rows, width), BF16),
        compiler_params=pltpu.CompilerParams(vmem_limit_bytes=14 << 20),
        cost_estimate=pl.CostEstimate(flops=2400000000, bytes_accessed=4 << 20, transcendentals=0),
    )(bits, near, near, far, far, weights, weights, stacks, gain)


def partner(value, mask):
    size = lax.axis_size("seq")
    return lax.ppermute(value, "seq", [(i, i ^ mask) for i in range(size)])


def order_pieces():
    return [p for i in range(PIECES) for p in (i, PIECES + i)]


def project(first_rows, make_last, out_weight):
    size = lax.axis_size("head")
    rows = first_rows.shape[0] // 2
    cols = out_weight.shape[1] // (2 * PIECES)
    ring = [[(j, (j + 1) % size) for j in range(size)], [(j, (j - 1) % size) for j in range(size)]]

    def term(block, piece):
        w = out_weight[:, piece * cols:(piece + 1) * cols]
        return jnp.dot(block, w, preferred_element_type=F32).astype(BF16)

    order = order_pieces()
    before, after = first_rows[:rows], first_rows[rows:]
    sums = {}
    for p in order:
        sums[p] = term(before if p < PIECES else after, p)
    last_rows = make_last()
    across, own_rows = last_rows[:rows], last_rows[rows:]
    sources = [(across, across), (after, before), (own_rows, own_rows)]
    last = None
    for s in range(size - 1):
        got, own = {}, {}
        for p in order:
            side = int(p >= PIECES)
            got[p] = lax.ppermute(sums[p], "head", ring[side])
            own[p] = term(sources[s][side], p)
        for p in order:
            keep = (own[p],) if last is None else (own[p], last)
            mine = lax.optimization_barrier(keep)[0]
            last = (got[p].astype(F32) + mine.astype(F32)).astype(BF16)
            sums[p] = last
    out = lax.optimization_barrier(jnp.zeros((rows, out_weight.shape[1]), BF16))
    for p in order:
        out = lax.dynamic_update_slice(out, sums[p], (0, p * cols))
    return out


def layer(queries, keys, values, log_decay, beta, level_weights, doc_start, norm_gain, out_weight):
    nbits = lax.axis_size("seq").bit_length() - 1
    blocks = lax.axis_size("head")
    index = lax.axis_index("seq")
    place = lax.axis_index("head")
    bits = jnp.stack([(index >> b) & 1 for b in range(nbits)] + [place]).astype(jnp.int32)
    gain = norm_gain.reshape(1, -1)
    in_hbm = lambda x: pltpu.with_memory_space_constraint(x, pltpu.HBM)
    given = [in_hbm(x) for x in (doc_start, queries, keys, values, log_decay, beta, level_weights)]
    heads = log_decay.shape[0]
    per = heads // (2 * CHUNKS)
    wide = jax.ShapeDtypeStruct((per, HEAD_DIM, 2 * HEAD_DIM), BF16)
    square = jax.ShapeDtypeStruct((per, HEAD_DIM, HEAD_DIM), BF16)
    near, far, maps = local_part(*given)
    sib = partner(maps, 1)
    curs = list(small_call(pair_kernel, bits, [maps, sib], [wide] * CHUNKS))
    carried = [None] * CHUNKS
    found = [[] for _ in range(CHUNKS)]
    packed = None
    for level in range(1, TOP):
        for c in range(CHUNKS):
            got = partner(curs[c], 1 << level)
            args = [got, curs[c]] if level == 1 else [got, curs[c], carried[c]]
            outs = [wide, square, square]
            packs = level == TOP - 1 and c == CHUNKS - 1
            if packs:
                args = [*found[0], *found[1], *args]
                outs = outs + [jax.ShapeDtypeStruct((CHUNKS * (TOP - 1) * per, HEAD_DIM, HEAD_DIM), BF16)]
            curs[c], x, carried[c], *packed = small_call(
                functools.partial(level_kernel, level, packs), bits, args, outs)
            found[c].append(x)
    got = [partner(curs[c][:, :, :HEAD_DIM], 1 << TOP) for c in range(CHUNKS)]
    top = small_call(top_kernel, bits, [*got, *carried],
                     [jax.ShapeDtypeStruct((CHUNKS * per, HEAD_DIM, HEAD_DIM), BF16)])[0]
    stacks = small_call(
        state_kernel, bits,
        [sib, packed[0], partner(packed[0], 1), top, partner(top, 1)],
        [jax.ShapeDtypeStruct((heads, (TOP + 1) * HEAD_DIM, HEAD_DIM), BF16)])[0]
    near, far = in_hbm(near), in_hbm(far)

    def read(offsets):
        return read_part(offsets, blocks, bits, near, far, given[6], stacks, gain)

    return project(read((blocks - 1, 1)), lambda: read((2, 0)), out_weight)


def solution(mesh):
    placed = (
        P("seq", "head"),
        P("seq", "head"),
        P("seq", "head"),
        P("head", "seq"),
        P("head", "seq"),
        P(None, "head", "seq"),
        P("seq"),
        P("head"),
        P("head", None),
    )
    return jax.shard_map(layer, mesh=mesh, in_specs=placed, out_specs=P(("seq", "head"), None), check_vma=False)
```
